256 devices in a mesh: box: 256 (over y, z, x, core).
Axes of the slice: x: 4, y: 4, z: 8, core: 2. Of those that a mesh axis runs over, the one named last changes fastest.
Arguments:
- sources: bfloat16 [128, 1048576], P(None, 'box'), may hold values from -6 to 6
- points: float32 [3, 1048576], P(None, 'box')
- near_list: int32 [2048, 12], P('box'), may hold values from 0 to 2047, as said below
- near_count: int32 [2048], P('box'), may hold values from 1 to 12
- far_list: int32 [2048, 4], P('box'), may hold values from 0 to 2047, as said below
- far_count: int32 [2048], P('box'), may hold values from 1 to 4
- leaf_basis: bfloat16 [2048, 64, 512], P('box'), may hold values from -0.25 to 0.25
- leaf_transfer: bfloat16 [256, 64, 512], P('box'), may hold values from -0.25 to 0.25
- leaf_coupling: bfloat16 [2048, 64, 256], P('box'), may hold values from -0.5 to 0.5
- branch_transfer: bfloat16 [256, 6, 64, 128], P('box'), may hold values from -1 to 1, as said below
- branch_coupling: bfloat16 [256, 7, 64, 256], P('box'), may hold values from -1 to 1, as said below
Outputs:
- field: float32 [128, 1048576], P(None, 'box')
The draws below stay inside these ranges and needn't reach their ends.
Inputs may be any that keep to these rules, and one draw needn't show every extreme that they name: `near_list`: row b lists near_count[b] distinct leaf boxes, the first b itself, the others within 12 of b in Morton order; entries from near_count[b] on hold b and are not used. `far_list`: row b lists far_count[b] distinct leaf boxes, each 2 to 12 from b in Morton order; entries from far_count[b] on hold b and are not used. branch_transfer[d, h] is equal for all d with the same d div 2^(h+1). branch_coupling[d, h] is equal for all d with the same d div 2^h.
All inputs are finite; a program needn't handle non-finite values.
Results may differ from the reference program's by a relative error of at most 0.0031.
Values may be sent and summed in bfloat16 or wider, within the bound.
A program may use at most 64 MiB of HBM per device.

```python
import math
import jax
import jax.numpy as jnp
from jax import lax

LEAF_DEV = 8
LEAF_PTS = 512
RANK = 64
NRHS = 128
NEAR_MAX = 12
FAR_MAX = 4
REACH = 12
DEV_BOXES = 256
LEAVES = 2048
POINTS = 1048576
UP_LEVELS = 6
FAR_LEVELS = 7


side_length = 2.0


corner_offset = 64.0


cloud_span = 3.0


cloud_shift = 1.0


def draw_points(key, part):
    leaf_of = jnp.arange(POINTS, dtype=jnp.int32) // LEAF_PTS
    bit_total = max(1, (LEAVES - 1).bit_length())
    cell_rows = []
    for axis_index in range(3):
        coordinate = jnp.zeros((POINTS,), jnp.int32)
        for bit_level in range((bit_total + 2) // 3):
            shifted = leaf_of >> 3 * bit_level + axis_index & 1
            coordinate = coordinate + (shifted << bit_level)
        cell_rows.append(coordinate)
    cell_grid = jnp.stack(cell_rows).astype(jnp.float32)
    within = jax.random.uniform(key, (3, POINTS), jnp.float32)
    within = cloud_span * within - cloud_shift
    return corner_offset + side_length * (cell_grid + within)


def pick_lists(score_key, leaf_ids, step_offsets, wanted):
    choice_total = step_offsets.shape[0]
    targets = leaf_ids[:, None] + step_offsets[None, :]
    inside = (targets >= 0) & (targets < LEAVES)
    scores = jax.random.randint(score_key, (LEAVES, choice_total), 0, 1 << 20) * choice_total + jnp.arange(choice_total, dtype=jnp.int32)
    scores = jnp.where(inside, scores, -1 - jnp.arange(choice_total, dtype=jnp.int32))
    ignored, picked = lax.top_k(scores, wanted)
    return jnp.take_along_axis(targets, picked, axis=1)


def near_tables(key):
    table_key = jax.random.fold_in(key, 11)
    heavy_key, pick_key, light_key, score_key = jax.random.split(table_key, 4)
    device_total = LEAVES // LEAF_DEV
    leaf_ids = jnp.arange(LEAVES, dtype=jnp.int32)
    heavy_device = jax.random.randint(heavy_key, (device_total,), 0, 4) == 0
    forced = jax.random.randint(pick_key, (), 0, device_total)
    heavy_device = heavy_device | (jnp.arange(device_total, dtype=jnp.int32) == forced)
    light_counts = jax.random.randint(light_key, (LEAVES,), 1, NEAR_MAX // 2 + 1)
    counts = jnp.where(heavy_device[leaf_ids // LEAF_DEV], NEAR_MAX, light_counts).astype(jnp.int32)
    step_offsets = jnp.concatenate([jnp.arange(-REACH, 0), jnp.arange(1, REACH + 1)]).astype(jnp.int32)
    chosen = pick_lists(score_key, leaf_ids, step_offsets, NEAR_MAX - 1)
    listing = jnp.concatenate([leaf_ids[:, None], chosen], axis=1)
    columns = jnp.arange(NEAR_MAX, dtype=jnp.int32)
    listing = jnp.where(columns[None, :] < counts[:, None], listing, leaf_ids[:, None])
    return (listing.astype(jnp.int32), counts)


def far_tables(key):
    table_key = jax.random.fold_in(key, 23)
    count_key, pick_key, score_key = jax.random.split(table_key, 3)
    leaf_ids = jnp.arange(LEAVES, dtype=jnp.int32)
    counts = jax.random.randint(count_key, (LEAVES,), 1, FAR_MAX + 1)
    forced = jax.random.randint(pick_key, (), 0, LEAVES)
    counts = jnp.where(leaf_ids == forced, FAR_MAX, counts).astype(jnp.int32)
    step_offsets = jnp.concatenate([jnp.arange(-REACH, -1), jnp.arange(2, REACH + 1)]).astype(jnp.int32)
    chosen = pick_lists(score_key, leaf_ids, step_offsets, FAR_MAX)
    columns = jnp.arange(FAR_MAX, dtype=jnp.int32)
    listing = jnp.where(columns[None, :] < counts[:, None], chosen, leaf_ids[:, None])
    return (listing.astype(jnp.int32), counts)


def draw_near_list(key, part):
    return near_tables(key)[0]


def draw_near_count(key, part):
    return near_tables(key)[1]


def draw_far_list(key, part):
    return far_tables(key)[0]


def draw_far_count(key, part):
    return far_tables(key)[1]


def random_block(sub_key, block_shape):
    return jax.random.normal(sub_key, block_shape, jnp.float32)


def draw_branch_transfer(key, part):
    stacks = []
    for height in range(UP_LEVELS):
        group_size = 2 ** (height + 1)
        block_shape = (DEV_BOXES // group_size, RANK, 2 * RANK)
        drawn = jnp.clip(random_block(jax.random.fold_in(key, 101 + height), block_shape) / math.sqrt(RANK), -1.0, 1.0)
        stacks.append(jnp.repeat(drawn, group_size, axis=0))
    return jnp.stack(stacks, axis=1).astype(jnp.bfloat16)


def draw_branch_coupling(key, part):
    stacks = []
    for height in range(FAR_LEVELS):
        group_size = 2 ** height
        block_shape = (DEV_BOXES // group_size, RANK, 4 * RANK)
        drawn = jnp.clip(random_block(jax.random.fold_in(key, 301 + height), block_shape) / math.sqrt(3 * RANK * group_size), -1.0, 1.0)
        stacks.append(jnp.repeat(drawn, group_size, axis=0))
    return jnp.stack(stacks, axis=1).astype(jnp.bfloat16)


def level_of(own_key, dims, shards, smallest, high):
    loudness = 1.0
    for axis_at, shards_of in shards:
        draws = jax.random.uniform(jax.random.fold_in(jax.random.fold_in(own_key, 6), axis_at), (shards_of,), jnp.float32, smallest / len(shards), high / len(shards))
        loudness = loudness * jnp.repeat(jnp.exp(draws), dims[axis_at] // shards_of).reshape((-1,) + (1,) * (len(dims) - 1 - axis_at))
    return loudness


def normal_values(stream_key, extent, scale, bound, cuts=(), held_as=jnp.bfloat16):
    loudness = level_of(stream_key, extent, cuts, -0.22, 0.18) if cuts else 1.0
    entries = jax.random.normal(stream_key, extent, jnp.float32) * scale * loudness
    return jnp.minimum(jnp.maximum(entries, -bound), bound).astype(held_as)


def setup_inputs(seed: int = 0) -> dict:
    key_of = jax.random.split(jax.random.key(seed), 12)
    sources = normal_values(key_of[0], (NRHS, POINTS), 1.0, 6.0, ((1, 256),))
    points = draw_points(jax.random.fold_in(key_of[11], 71), 0)
    near_list = draw_near_list(jax.random.fold_in(key_of[11], 71), 0)
    near_count = draw_near_count(jax.random.fold_in(key_of[11], 71), 0)
    far_list = draw_far_list(jax.random.fold_in(key_of[11], 71), 0)
    far_count = draw_far_count(jax.random.fold_in(key_of[11], 71), 0)
    leaf_basis = normal_values(key_of[6], (LEAVES, RANK, LEAF_PTS), LEAF_PTS ** -0.5, 0.25, ((0, 256),))
    leaf_transfer = normal_values(key_of[7], (DEV_BOXES, RANK, LEAF_DEV * RANK), (RANK * LEAF_DEV) ** -0.5, 0.25, ((0, 256),))
    leaf_coupling = normal_values(key_of[8], (LEAVES, RANK, FAR_MAX * RANK), (2 * RANK) ** -0.5, 0.5, ((0, 256),))
    branch_transfer = draw_branch_transfer(jax.random.fold_in(key_of[11], 71), 0)
    branch_coupling = draw_branch_coupling(jax.random.fold_in(key_of[11], 71), 0)
    return dict(sources=sources, points=points, near_list=near_list, near_count=near_count, far_list=far_list, far_count=far_count, leaf_basis=leaf_basis, leaf_transfer=leaf_transfer, leaf_coupling=leaf_coupling, branch_transfer=branch_transfer, branch_coupling=branch_coupling)


softening = 0.25
inverse_sphere = 0.07957747154594767
highest = lax.Precision.HIGHEST
far_offsets = (-3, -2, 2, 3)

def kernel_block(source_points, target_points):
    gap_x = source_points[0][:, None] - target_points[0][None, :]
    gap_y = source_points[1][:, None] - target_points[1][None, :]
    gap_z = source_points[2][:, None] - target_points[2][None, :]
    squared = gap_x * gap_x + gap_y * gap_y + gap_z * gap_z
    return (inverse_sphere / jnp.sqrt(squared + softening)).astype(jnp.bfloat16)

def reference(sources, points, near_list, near_count, far_list, far_count, leaf_basis, leaf_transfer, leaf_coupling, branch_transfer, branch_coupling):
    source_leaves = sources.reshape(NRHS, LEAVES, LEAF_PTS)
    leaf_points = points.reshape(3, LEAVES, LEAF_PTS)

    def near_leaf(packed):
        target, listing, used_count = packed
        target_points = leaf_points[:, target]

        def add_one(column, totals):
            source = listing[column]
            kernel = kernel_block(leaf_points[:, source], target_points)
            return totals + jnp.dot(source_leaves[:, source], kernel, preferred_element_type=jnp.float32)
        return lax.fori_loop(0, used_count, add_one, jnp.zeros((NRHS, LEAF_PTS), jnp.float32))
    near_sum = lax.map(near_leaf, (jnp.arange(LEAVES, dtype=jnp.int32), near_list, near_count))
    moments = jnp.einsum('brp,nbp->brn', leaf_basis.astype(jnp.float32), source_leaves.astype(jnp.float32), precision=highest).astype(jnp.bfloat16)
    stacked_leaves = moments.reshape(DEV_BOXES, LEAF_DEV * RANK, NRHS).astype(jnp.float32)
    device_moment = jnp.einsum('arq,aqn->arn', leaf_transfer.astype(jnp.float32), stacked_leaves, precision=highest)
    levels = [device_moment]
    current = device_moment
    for height in range(UP_LEVELS):
        stride = 2 ** (height + 1)
        joined = branch_transfer[::stride, height].astype(jnp.float32)
        left_part = jnp.einsum('arq,aqn->arn', joined[:, :, :RANK], current[0::2], precision=highest)
        right_part = jnp.einsum('arq,aqn->arn', joined[:, :, RANK:], current[1::2], precision=highest)
        current = left_part + right_part
        levels.append(current)
    far_terms = []
    for height in range(FAR_LEVELS):
        count_boxes = DEV_BOXES // 2 ** height
        box_ids = jnp.arange(count_boxes, dtype=jnp.int32)
        level_moment = levels[height]
        received = []
        for offset in far_offsets:
            neighbour = box_ids + offset
            usable = (neighbour >= 0) & (neighbour < count_boxes)
            if offset == -3:
                usable = usable & (box_ids % 2 == 1)
            if offset == 3:
                usable = usable & (box_ids % 2 == 0)
            picked_rows = level_moment[jnp.clip(neighbour, 0, count_boxes - 1)]
            received.append(jnp.where(usable[:, None, None], picked_rows, jnp.zeros((), jnp.float32)))
        coupling = branch_coupling[::2 ** height, height].astype(jnp.float32)
        far_terms.append(jnp.einsum('arq,aqn->arn', coupling, jnp.concatenate(received, axis=1), precision=highest))
    local_field = far_terms[FAR_LEVELS - 1]
    for height in range(FAR_LEVELS - 2, -1, -1):
        stride = 2 ** (height + 1)
        joined = branch_transfer[::stride, height].astype(jnp.float32)
        down_left = jnp.einsum('arq,arn->aqn', joined[:, :, :RANK], local_field, precision=highest)
        down_right = jnp.einsum('arq,arn->aqn', joined[:, :, RANK:], local_field, precision=highest)
        alternated = jnp.stack([down_left, down_right], axis=1).reshape(-1, RANK, NRHS)
        local_field = far_terms[height] + alternated
    spread_down = jnp.einsum('arq,arn->aqn', leaf_transfer.astype(jnp.float32), local_field, precision=highest).reshape(LEAVES, RANK, NRHS)
    far_rows = moments[far_list]
    far_live = jnp.arange(FAR_MAX, dtype=jnp.int32)[None, :] < far_count[:, None]
    far_rows = jnp.where(far_live[:, :, None, None], far_rows, jnp.zeros((), jnp.bfloat16))
    far_rows = far_rows.reshape(LEAVES, FAR_MAX * RANK, NRHS).astype(jnp.float32)
    leaf_far = jnp.einsum('brq,bqn->brn', leaf_coupling.astype(jnp.float32), far_rows, precision=highest)
    leaf_local = (leaf_far + spread_down).astype(jnp.bfloat16)
    far_field = jnp.einsum('brn,brp->bnp', leaf_local.astype(jnp.float32), leaf_basis.astype(jnp.float32), precision=highest)
    combined = near_sum + far_field
    return combined.transpose(1, 0, 2).reshape(NRHS, POINTS).astype(jnp.float32)
```

```python
import functools

import jax
import jax.numpy as jnp
from jax import lax
from jax.experimental import pallas as pl
from jax.experimental.pallas import tpu as pltpu
from jax.sharding import PartitionSpec as P

F32 = jnp.float32
BF16 = jnp.bfloat16
SOFT = 0.25
INV = 0.07957747154594767
SCALE = 1.0 / INV
EXTENT = 1024.0 * SCALE * SCALE
FAR_SCALE = 1e-27
LEAF = 8
PTS = 512
RANK = 64
RHS = 128
NEAR = 12
FAR = 4
REACH = 12
SLOTS = LEAF + 2 * REACH
OWN = REACH
UP = 6
LEVELS = 7
FEAT = 32
GROUP = 6
MESH = pl.DeviceIdType.MESH

WINDOW = (
    (1, 6, 2, 0),
    (-1, 0, 2, 0),
    (1, 4, 2, 1),
    (-1, 2, 2, 1),
    (2, 4, 4, 2),
    (-2, 0, 4, 2),
    (1, 0, 4, 2),
    (-1, 4, 4, 2),
)
EDGES = ((1, 0, 8), (-1, 0, 8), (2, 4, 4), (-2, 0, 4))
N_WIN, N_EDGE = len(WINDOW), len(EDGES)
I_PTS = 0
I_MOM = I_PTS + N_EDGE
I_WIN = I_MOM + N_EDGE
I_SWAP = I_WIN + N_WIN
I_FAR = I_SWAP + UP
N_MSG = I_FAR + 3 * LEVELS

UP_AT = (0, 1, 3, 5, 7, 10)
FAR_AT = (11, 11, 12, 12, 13, 14)


def split3(x):
    a = x.astype(BF16)
    r = x - a.astype(F32)
    b = r.astype(BF16)
    return a, b, (r - b.astype(F32)).astype(BF16)


def rows(parts):
    return jnp.concatenate(parts, axis=0)


def source_features(x):
    n = jnp.sum(x * x, axis=0, keepdims=True)
    a, b, c = split3(x)
    n0, n1, n2 = split3(n + SOFT * SCALE * SCALE)
    ones = jnp.ones((3, PTS), BF16)
    return rows([a, b, a, b, c, a, n0, n1, n2, ones, jnp.zeros((FEAT - 24, PTS), BF16)]), n


def target_features(x):
    n = jnp.sum(x * x, axis=0, keepdims=True)
    a, b, c = split3(-2.0 * x)
    n0, n1, n2 = split3(n)
    ones = jnp.ones((3, PTS), BF16)
    return rows([a, a, b, b, a, c, ones, n0, n1, n2, jnp.zeros((FEAT - 24, PTS), BF16)])


def exact_dot(left, right, contract=1):
    high = right.astype(BF16)
    low = (right - high.astype(F32)).astype(BF16)
    both = lax.dot_general(
        left,
        jnp.concatenate([high, low], axis=1),
        (((contract,), (0,)), ((), ())),
        preferred_element_type=F32,
    )
    return both[:, :RHS] + both[:, RHS:]


def tree_kernel(
    devices,
    near_list,
    near_count,
    far_list,
    far_count,
    sources,
    points,
    basis_in,
    leaf_transfer_in,
    coupling_in,
    branch_transfer_in,
    branch_coupling_in,
    field,
    leaf_local_out,
    norms_out,
    charges_out,
    points_out,
    charges,
    pts,
    moments,
    feats,
    kernels,
    basis,
    transfer,
    coupling,
    branch_t,
    branch_c,
    level,
    term,
    swapped,
    arrived,
    far,
    spread,
    norms,
    leaf_local,
    out_buf,
    load_sem,
    store_sem,
    send_sem,
    recv_sem,
):
    me = lax.axis_index("box")

    def other(distance):
        return lax.rem(me + distance + devices, devices)

    def third(height):
        odd = lax.rem(lax.div(me, 1 << height), 2)
        return other((3 - 6 * odd) * (1 << height))

    def remote(index, src, dst, device):
        return pltpu.make_async_remote_copy(
            src_ref=src,
            dst_ref=dst,
            send_sem=send_sem.at[index],
            recv_sem=recv_sem.at[index],
            device_id=(device,),
            device_id_type=MESH,
        )

    barrier = pltpu.get_barrier_semaphore()
    partners = [other(s * (1 << k)) for k in range(LEVELS) for s in (1, -1)]
    partners += [other(devices // 2)] + [third(h) for h in range(LEVELS)]
    for partner in partners:
        pl.semaphore_signal(barrier, inc=1, device_id=(partner,), device_id_type=MESH)

    loads = []

    def load(src, dst):
        copy = pltpu.make_async_copy(src, dst, load_sem.at[len(loads)])
        copy.start()
        loads.append(copy)
        return copy

    load_points = [load(points.at[:, pl.ds(i * PTS, PTS)], pts.at[OWN + i]) for i in range(LEAF)]
    load_charges = [
        load(sources.at[:, pl.ds(i * PTS, PTS)], charges.at[OWN + i]) for i in range(LEAF)
    ]
    load_basis = load(basis_in, basis)
    load_transfer = load(leaf_transfer_in.at[0], transfer)
    load_branch_t = load(branch_transfer_in.at[0], branch_t)
    load_branch_c = load(branch_coupling_in.at[0], branch_c)
    load_coupling = load(coupling_in, coupling)

    def edge(base, buf, which):
        distance, first, count = EDGES[which]
        return remote(
            base + which,
            buf.at[pl.ds(OWN + first, count)],
            buf.at[pl.ds(OWN + first - LEAF * distance, count)],
            other(distance),
        )

    def window(which):
        distance, first, count, _ = WINDOW[which]
        return remote(
            I_WIN + which,
            charges.at[pl.ds(OWN + first, count)],
            charges.at[pl.ds(OWN + first - LEAF * distance, count)],
            other(distance),
        )

    def window_stage(stage):
        for which in range(N_WIN):
            if WINDOW[which][3] == stage:
                window(which).start()

    def swap(height):
        bit = lax.rem(lax.div(me, 1 << height), 2)
        return remote(
            I_SWAP + height,
            term.at[height],
            swapped.at[height],
            me + (1 - 2 * bit) * (1 << height),
        )

    def far_copies(height):
        step = 1 << height
        copies = []
        for slot, device in ((0, other(2 * step)), (1, other(-2 * step)), (2, third(height))):
            if height == LEVELS - 1 and slot == 1:
                continue
            copies.append(
                remote(I_FAR + 3 * height + slot, level.at[height], arrived.at[height, slot], device)
            )
        return copies

    def half(height):
        bit = lax.rem(lax.div(me, 1 << height), 2)
        joined = branch_t[height].astype(F32)
        return jnp.where(bit == 1, joined[:, RANK:], joined[:, :RANK]).astype(BF16)

    for copy in load_points:
        copy.wait()
    pl.semaphore_wait(barrier, len(partners))
    for which in range(N_EDGE):
        edge(I_PTS, pts, which).start()
    for copy in load_charges:
        copy.wait()
    window_stage(0)

    load_basis.wait()
    load_transfer.wait()
    for i in range(LEAF):
        moments[OWN + i] = lax.dot_general(
            basis[i], charges[OWN + i], (((1,), (1,)), ((), ())), preferred_element_type=F32
        ).astype(BF16)
    level[0] = jnp.dot(
        transfer[...],
        moments[pl.ds(OWN, LEAF)].reshape(LEAF * RANK, RHS),
        preferred_element_type=F32,
    )
    load_branch_t.wait()
    term[0] = exact_dot(half(0), level[0])
    swap(0).start()
    for which in range(N_EDGE):
        edge(I_MOM, moments, which).start()
    for copy in far_copies(0):
        copy.start()

    def prepare(slot):
        x = pts[slot]
        centred = (x - x[:, 0:1]) * SCALE
        packed, own_norm = source_features(centred)
        feats[slot] = packed.astype(F32).T.astype(BF16)
        apart = (x - pts[OWN][:, 0:1]) * SCALE
        apart_norm = jnp.sum(apart * apart, axis=0, keepdims=True) * FAR_SCALE
        norms[pl.ds(slot, 1)] = jnp.maximum(own_norm, apart_norm)

    def prepare_pair(i, carry):
        prepare(2 * i)
        prepare(2 * i + 1)
        return carry

    lax.fori_loop(OWN // 2, (OWN + LEAF) // 2, prepare_pair, 0)
    for which in range(N_EDGE):
        edge(I_PTS, pts, which).wait_recv()
    lax.fori_loop(0, OWN // 2, prepare_pair, 0)
    lax.fori_loop((OWN + LEAF) // 2, SLOTS // 2, prepare_pair, 0)

    def slot_of(entry):
        return jnp.clip(entry - me * LEAF + OWN, 0, SLOTS - 1)

    def build(leaf, column):
        slot = slot_of(near_list[leaf, column])
        target = (pts[OWN + leaf] - pts[slot][:, 0:1]) * SCALE
        squared = jnp.dot(feats[slot], target_features(target), preferred_element_type=F32)
        kernels[leaf * NEAR + column] = lax.rsqrt(
            jnp.maximum(squared, SOFT * SCALE * SCALE)
        ).astype(BF16)

    def up_step(height):
        swap(height).wait_recv()
        level[height + 1] = term[height] + swapped[height]
        if height + 1 < UP:
            term[height + 1] = exact_dot(half(height + 1), level[height + 1])
            swap(height + 1).start()
        for copy in far_copies(height + 1):
            copy.start()
        if height < 2:
            window_stage(height + 1)

    def far_step(height):
        for copy in far_copies(height):
            copy.wait_recv()
        index = lax.div(me, 1 << height)
        total = devices >> height
        odd = lax.rem(index, 2)

        def kept(slot, usable):
            return jnp.where(usable, arrived[height, slot], 0.0)

        last = 0 if height == LEVELS - 1 else 1
        stack = rows(
            [
                kept(2, (odd == 1) & (index >= 3)),
                kept(0, index >= 2),
                kept(last, index + 2 < total),
                kept(2, (odd == 0) & (index + 3 < total)),
            ]
        )
        far[height] = exact_dot(branch_c[height], stack)

    def near_group(group, carry):
        leaf = lax.div(group, NEAR // GROUP)
        first = lax.rem(group, NEAR // GROUP) * GROUP
        for u in range(GROUP):
            build(leaf, first + u)
        for height, at in enumerate(UP_AT):

            @pl.when(group == at)
            def _():
                up_step(height)

        for height, at in enumerate(FAR_AT):

            @pl.when(group == at)
            def _():
                if height == 0:
                    load_branch_c.wait()
                far_step(height)

        return carry

    lax.fori_loop(0, LEAF * NEAR // GROUP, near_group, 0)

    far_step(LEVELS - 1)
    local = far[LEVELS - 1]
    for height in range(UP - 1, -1, -1):
        local = far[height] + exact_dot(half(height), local, 0)
    spread[...] = exact_dot(transfer[...], local, 0).reshape(LEAF, RANK, RHS)
    load_coupling.wait()
    for which in range(N_EDGE):
        edge(I_MOM, moments, which).wait_recv()
    for which in range(N_WIN):
        window(which).wait_recv()
    keep = [
        pltpu.make_async_copy(charges, charges_out, store_sem.at[2]),
        pltpu.make_async_copy(pts, points_out, store_sem.at[3]),
        pltpu.make_async_copy(norms, norms_out, store_sem.at[4]),
    ]
    for copy in keep:
        copy.start()

    def out_copy(leaf, buf):
        return pltpu.make_async_copy(
            out_buf.at[buf], field.at[:, pl.ds(pl.multiple_of(leaf * PTS, PTS), PTS)], store_sem.at[buf]
        )

    def finish(leaf, buf):
        blocks = []
        for j in range(FAR):
            block = moments[slot_of(far_list[leaf, j])]
            blocks.append(jnp.where(j < far_count[leaf], block.astype(F32), 0.0).astype(BF16))
        here = jnp.dot(coupling[leaf], rows(blocks), preferred_element_type=F32) + spread[leaf]
        here = here.astype(BF16)
        leaf_local[leaf] = here
        total = lax.dot_general(
            here, basis[leaf], (((0,), (0,)), ((), ())), preferred_element_type=F32
        )
        for j in range(NEAR):
            block = charges[slot_of(near_list[leaf, j])]
            block = jnp.where(j < near_count[leaf], block, jnp.zeros_like(block))
            total += jnp.dot(block, kernels[leaf * NEAR + j], preferred_element_type=F32)
        out_buf[buf] = total
        out_copy(leaf, buf).start()

    def finish_pair(i, carry):
        for buf in range(2):

            @pl.when(i > 0)
            def _():
                out_copy(2 * i - 2 + buf, buf).wait()

            finish(2 * i + buf, buf)
        return carry

    lax.fori_loop(0, LEAF // 2, finish_pair, 0)
    out_copy(LEAF - 2, 0).wait()
    out_copy(LEAF - 1, 1).wait()
    keep.append(pltpu.make_async_copy(leaf_local, leaf_local_out, store_sem.at[5]))
    keep[-1].start()
    for copy in keep:
        copy.wait()
    for which in range(N_EDGE):
        edge(I_PTS, pts, which).wait_send()
        edge(I_MOM, moments, which).wait_send()
    for which in range(N_WIN):
        window(which).wait_send()
    for height in range(UP):
        swap(height).wait_send()
    for height in range(LEVELS):
        for copy in far_copies(height):
            copy.wait_send()


N_LOAD = 2 * LEAF + 5


def tree(devices, *operands):
    any_spec = pl.BlockSpec(memory_space=pl.ANY)
    smem_spec = pl.BlockSpec(memory_space=pltpu.SMEM)
    return pl.pallas_call(
        functools.partial(tree_kernel, devices),
        out_shape=(
            jax.ShapeDtypeStruct((RHS, LEAF * PTS), F32),
            jax.ShapeDtypeStruct((LEAF, RANK, RHS), BF16),
            jax.ShapeDtypeStruct((SLOTS, PTS), F32),
            jax.ShapeDtypeStruct((SLOTS, RHS, PTS), BF16),
            jax.ShapeDtypeStruct((SLOTS, 3, PTS), F32),
        ),
        in_specs=[smem_spec] * 4 + [any_spec] * 7,
        out_specs=(any_spec,) * 5,
        scratch_shapes=[
            pltpu.VMEM((SLOTS, RHS, PTS), BF16),
            pltpu.VMEM((SLOTS, 3, PTS), F32),
            pltpu.VMEM((SLOTS, RANK, RHS), BF16),
            pltpu.VMEM((SLOTS, PTS, FEAT), BF16),
            pltpu.VMEM((LEAF * NEAR, PTS, PTS), BF16),
            pltpu.VMEM((LEAF, RANK, PTS), BF16),
            pltpu.VMEM((RANK, LEAF * RANK), BF16),
            pltpu.VMEM((LEAF, RANK, FAR * RANK), BF16),
            pltpu.VMEM((UP, RANK, 2 * RANK), BF16),
            pltpu.VMEM((LEVELS, RANK, 4 * RANK), BF16),
            pltpu.VMEM((LEVELS, RANK, RHS), F32),
            pltpu.VMEM((UP, RANK, RHS), F32),
            pltpu.VMEM((UP, RANK, RHS), F32),
            pltpu.VMEM((LEVELS, 3, RANK, RHS), F32),
            pltpu.VMEM((LEVELS, RANK, RHS), F32),
            pltpu.VMEM((LEAF, RANK, RHS), F32),
            pltpu.VMEM((SLOTS, PTS), F32),
            pltpu.VMEM((LEAF, RANK, RHS), BF16),
            pltpu.VMEM((2, RHS, PTS), F32),
            pltpu.SemaphoreType.DMA((N_LOAD,)),
            pltpu.SemaphoreType.DMA((6,)),
            pltpu.SemaphoreType.DMA((N_MSG,)),
            pltpu.SemaphoreType.DMA((N_MSG,)),
        ],
        compiler_params=pltpu.CompilerParams(
            collective_id=0, has_side_effects=True, vmem_limit_bytes=66_000_000
        ),
        name="tree",
    )(*operands)


def result_kernel(
    near_list, near_count, norms, fast, leaf_local, charges, points, basis, field,
    buf, charge_buf, point_buf, local_buf, basis_buf, in_sem, out_sem, sem,
):
    fits = jnp.max(norms[...]) <= EXTENT
    bad = jnp.max(jnp.where(norms[...] <= EXTENT, 0.0, 1.0)) > 0.0
    direct = jnp.logical_or(bad, jnp.logical_not(fits))

    def cols(leaf):
        return pl.ds(leaf * PTS, PTS)

    @pl.when(jnp.logical_not(direct))
    def _():
        reads = [
            pltpu.make_async_copy(fast.at[:, cols(i)], buf.at[i], in_sem.at[i]) for i in range(LEAF)
        ]
        writes = [
            pltpu.make_async_copy(buf.at[i], field.at[:, cols(i)], out_sem.at[i]) for i in range(LEAF)
        ]
        for copy in reads:
            copy.start()
        for read, write in zip(reads, writes):
            read.wait()
            write.start()
        for write in writes:
            write.wait()

    @pl.when(direct)
    def _():
        me = lax.axis_index("box")

        def fetch(src, dst):
            copy = pltpu.make_async_copy(src, dst, sem)
            copy.start()
            copy.wait()

        fetch(points, point_buf)
        fetch(leaf_local, local_buf)
        fetch(basis, basis_buf)

        def one(leaf, carry):
            buf[0] = lax.dot_general(
                local_buf[leaf], basis_buf[leaf], (((0,), (0,)), ((), ())), preferred_element_type=F32
            )
            target = point_buf[OWN + leaf]

            def pair(j, inner):
                slot = jnp.clip(near_list[leaf, j] - me * LEAF + OWN, 0, SLOTS - 1)
                fetch(charges.at[slot], charge_buf)
                column = point_buf[slot].T
                squared = SOFT
                for axis in range(3):
                    gap = column[:, axis : axis + 1] - target[axis : axis + 1]
                    squared = squared + gap * gap
                block = (INV * lax.rsqrt(squared)).astype(BF16)
                buf[0] += jnp.dot(charge_buf[...], block, preferred_element_type=F32)
                return inner

            lax.fori_loop(0, near_count[leaf], pair, 0)
            fetch(buf.at[0], field.at[:, pl.ds(pl.multiple_of(leaf * PTS, PTS), PTS)])
            return carry

        lax.fori_loop(0, LEAF, one, 0)


def result(*operands):
    any_spec = pl.BlockSpec(memory_space=pl.ANY)
    smem_spec = pl.BlockSpec(memory_space=pltpu.SMEM)
    vmem_spec = pl.BlockSpec(memory_space=pltpu.VMEM)
    return pl.pallas_call(
        result_kernel,
        out_shape=jax.ShapeDtypeStruct((RHS, LEAF * PTS), F32),
        in_specs=[smem_spec] * 2 + [vmem_spec] + [any_spec] * 5,
        out_specs=any_spec,
        scratch_shapes=[
            pltpu.VMEM((LEAF, RHS, PTS), F32),
            pltpu.VMEM((RHS, PTS), BF16),
            pltpu.VMEM((SLOTS, 3, PTS), F32),
            pltpu.VMEM((LEAF, RANK, RHS), BF16),
            pltpu.VMEM((LEAF, RANK, PTS), BF16),
            pltpu.SemaphoreType.DMA((LEAF,)),
            pltpu.SemaphoreType.DMA((LEAF,)),
            pltpu.SemaphoreType.DMA,
        ],
        name="result",
    )(*operands)


def on_device(
    sources, points, near_list, near_count, far_list, far_count,
    leaf_basis, leaf_transfer, leaf_coupling, branch_transfer, branch_coupling,
):
    devices = lax.axis_size("box")
    fast, leaf_local, norms, charges, window_points = tree(
        devices, near_list, near_count, far_list, far_count, sources, points,
        leaf_basis, leaf_transfer, leaf_coupling, branch_transfer, branch_coupling,
    )
    return result(
        near_list, near_count, norms, fast, leaf_local, charges, window_points, leaf_basis
    )


def solution(mesh):
    placed = (
        P(None, "box"),
        P(None, "box"),
        P("box", None),
        P("box"),
        P("box", None),
        P("box"),
        P("box", None, None),
        P("box", None, None),
        P("box", None, None),
        P("box", None, None, None),
        P("box", None, None, None),
    )
    return jax.shard_map(
        on_device, mesh=mesh, in_specs=placed, out_specs=P(None, "box"), check_vma=False
    )
```

```python
import functools

import jax
import jax.numpy as jnp
from jax import lax
from jax.experimental import pallas as pl
from jax.experimental.pallas import tpu as pltpu
from jax.sharding import PartitionSpec as P

F32 = jnp.float32
BF16 = jnp.bfloat16
SOFT = 0.25
INV = 0.07957747154594767
SCALE = 1.0 / INV
EXTENT = 1024.0 * SCALE * SCALE
FAR_SCALE = 1e-27
LEAF = 8
PTS = 512
RANK = 64
RHS = 128
NEAR = 12
FAR = 4
REACH = 12
SLOTS = LEAF + 2 * REACH
OWN = REACH
UP = 6
LEVELS = 7
FEAT = 48
GROUP = 6
MESH = pl.DeviceIdType.MESH

EDGES = ((1, 0, 8), (-1, 0, 8), (2, 4, 4), (-2, 0, 4))
N_EDGE = len(EDGES)
NEST = 3
PAIR = (6, 24, 40, 48, 56)
I_PTS = 0
I_MOM = I_PTS + N_EDGE
I_WIN = I_MOM + N_EDGE
I_CORE = I_WIN + 5
I_LINE = I_CORE + 1
I_COLUMN = I_LINE + 3
I_FAR = I_COLUMN + 7
N_MSG = I_FAR + 3 * LEVELS

CORE_AT, LINE_AT, COLUMN_AT, PASS_AT = 0, 3, 8, 5
FAR_AT = (9, 10, 14, 11, 14, 15)


def split3(x):
    a = x.astype(BF16)
    r = x - a.astype(F32)
    b = r.astype(BF16)
    return a, b, (r - b.astype(F32)).astype(BF16)


def rows(parts):
    return jnp.concatenate(parts, axis=0)


def halves(x):
    high = x.astype(BF16)
    return high, (x - high.astype(F32)).astype(BF16)


def features(x, of_source):
    row = lax.broadcasted_iota(jnp.int32, x.shape, 0)
    n = jnp.sum(x * x, axis=0, keepdims=True)
    a, b, c = (v.astype(F32) for v in split3(x if of_source else -2.0 * x))
    n0, n1, n2 = (v.astype(F32) for v in split3(n + SOFT * SCALE * SCALE if of_source else n))
    norm = jnp.where(row == 3, n0, jnp.where(row == 4, n1, jnp.where(row == 5, n2, 0.0)))
    ones = jnp.where((row >= 3) & (row < 6), 1.0, 0.0)
    if of_source:
        parts = [a + norm, b + ones, a, b, c, a]
    else:
        parts = [a + ones, a + norm, b, b, a, c]
    return rows(parts), n


def exact_dot(left, right):
    width = right.shape[1]
    both = jnp.dot(left, jnp.concatenate(halves(right), axis=1), preferred_element_type=F32)
    return both[:, :width] + both[:, width:]


def tree_kernel(
    devices,
    near_list,
    near_count,
    far_list,
    far_count,
    sources,
    points,
    basis_in,
    leaf_transfer_in,
    coupling_in,
    branch_transfer_in,
    branch_coupling_in,
    field,
    leaf_local_out,
    norms_out,
    charges_out,
    points_out,
    charges,
    pts,
    moments,
    feats,
    padded,
    kernels,
    basis,
    transfer,
    coupling,
    branch_t,
    branch_c,
    ladder,
    level,
    core_out,
    core_in,
    line_out,
    line_in,
    column_own,
    column_out,
    column_in,
    arrived,
    far,
    spread,
    norms,
    leaf_local,
    out_buf,
    load_sem,
    store_sem,
    send_sem,
    recv_sem,
):
    me = lax.axis_index("box")

    def other(distance):
        return lax.rem(me + distance + devices, devices)

    def flipped(pattern):
        return lax.bitwise_xor(me, pattern)

    odd_core = lax.rem(me, 2)
    sibling = me + 1 - 2 * odd_core

    def third(height):
        odd = lax.rem(lax.div(me, 1 << height), 2)
        return other((3 - 6 * odd) * (1 << height))

    def remote(index, src, dst, device):
        return pltpu.make_async_remote_copy(
            src_ref=src,
            dst_ref=dst,
            send_sem=send_sem.at[index],
            recv_sem=recv_sem.at[index],
            device_id=(device,),
            device_id_type=MESH,
        )

    barrier = pltpu.get_barrier_semaphore()
    partners = [other(s * (1 << k)) for k in range(LEVELS) for s in (1, -1)]
    partners += [other(devices // 2)] + [third(h) for h in range(LEVELS)]
    partners += [flipped(pattern) for pattern in PAIR]
    for partner in partners:
        pl.semaphore_signal(barrier, inc=1, device_id=(partner,), device_id_type=MESH)

    loads = []

    def load(src, dst):
        copy = pltpu.make_async_copy(src, dst, load_sem.at[len(loads)])
        copy.start()
        loads.append(copy)
        return copy

    load_points = [load(points.at[:, pl.ds(i * PTS, PTS)], pts.at[OWN + i]) for i in range(LEAF)]
    load_charges = [
        load(sources.at[:, pl.ds(i * PTS, PTS)], charges.at[OWN + i]) for i in range(LEAF)
    ]
    load_basis = load(basis_in, basis)
    load_transfer = load(leaf_transfer_in.at[0], transfer)
    load_branch_t = load(branch_transfer_in.at[0], branch_t)
    load_branch_c = load(branch_coupling_in.at[0], branch_c)
    load_coupling = load(coupling_in, coupling)

    def edge(base, buf, which):
        distance, first, count = EDGES[which]
        return remote(
            base + which,
            buf.at[pl.ds(OWN + first, count)],
            buf.at[pl.ds(OWN + first - LEAF * distance, count)],
            other(distance),
        )

    def window(which):
        def four(index, first, there, device, count=4):
            return remote(
                I_WIN + index, charges.at[pl.ds(first, count)], charges.at[pl.ds(there, count)], device
            )

        if which == 0:
            return four(0, OWN, 4 + 16 * odd_core, sibling, LEAF)
        beyond = other(2 * odd_core - 1)
        if which == 1:
            return four(1, OWN + 4 * odd_core, 20 - 12 * odd_core, beyond)
        if which == 2:
            return four(2, OWN + 4 - 4 * odd_core, 24 - 20 * odd_core, beyond)
        if which == 3:
            return four(3, OWN + 4 - 4 * odd_core, 28 * odd_core, other(2 - 4 * odd_core))
        return four(4, 8 + 12 * odd_core, 28 * odd_core, sibling)

    def core_copy():
        return remote(I_CORE, core_out, core_in, sibling)

    def line_copies():
        return [
            remote(I_LINE, line_out, line_in.at[pl.ds(0, 2)], flipped(2)),
            remote(I_LINE + 1, line_out.at[1], line_in.at[2], flipped(4)),
            remote(I_LINE + 2, line_out.at[1], line_in.at[3], flipped(6)),
        ]

    def column_first(k):
        return 0 if k == 1 else 1 if k < 4 else 2

    def column_copies():
        copies = []
        for k in range(1, 8):
            part = pl.ds(column_first(k), NEST - column_first(k))
            copies.append(
                remote(
                    I_COLUMN + k - 1, column_out.at[part], column_in.at[k - 1, part], flipped(8 * k)
                )
            )
        return copies

    def far_copies(height):
        step = 1 << height
        copies = []
        for slot, device in ((0, other(2 * step)), (1, other(-2 * step)), (2, third(height))):
            if height == LEVELS - 1 and slot == 1:
                continue
            copies.append(
                remote(I_FAR + 3 * height + slot, level.at[height], arrived.at[height, slot], device)
            )
        return copies

    def half(height):
        bit = lax.rem(lax.div(me, 1 << height), 2)
        joined = branch_t[height].astype(F32)
        return jnp.where(bit == 1, joined[:, RANK:], joined[:, :RANK]).astype(BF16)

    for copy in load_points:
        copy.wait()
    pl.semaphore_wait(barrier, len(partners))
    for which in range(N_EDGE):
        edge(I_PTS, pts, which).start()
    for copy in load_charges:
        copy.wait()
    window(1).start()
    window(0).start()

    load_basis.wait()
    load_transfer.wait()
    load_branch_t.wait()
    for i in range(LEAF):
        moments[OWN + i] = lax.dot_general(
            basis[i], charges[OWN + i], (((1,), (1,)), ((), ())), preferred_element_type=F32
        ).astype(BF16)
    base = jnp.dot(
        transfer[...],
        moments[pl.ds(OWN, LEAF)].reshape(LEAF * RANK, RHS),
        preferred_element_type=F32,
    )
    for nest in range(2):
        first, second, last = (half(NEST * nest + i) for i in range(NEST))
        two = jnp.dot(second, first, preferred_element_type=F32)
        three = exact_dot(last, two)
        high, low = halves(rows([first.astype(F32), two, three]))
        ladder[nest] = jnp.concatenate([high, low], axis=1)

    def climb(nest, x):
        high, low = halves(x)
        pair = ladder[nest]
        wide = jnp.concatenate([high, low], axis=1)
        r = jnp.dot(pair[:, :RANK], wide, preferred_element_type=F32)
        fine = jnp.dot(pair[:, RANK:], high, preferred_element_type=F32)
        return (r[:, :RHS] + r[:, RHS:] + fine).reshape(NEST, RANK, RHS)

    def descend(nest, x):
        wide = jnp.concatenate(halves(x), axis=1)
        r = lax.dot_general(
            ladder[nest], wide, (((0,), (0,)), ((), ())), preferred_element_type=F32
        )
        return r[:RANK, :RHS] + r[:RANK, RHS:] + r[RANK:, :RHS]

    core_out[...] = climb(0, base)
    level[0] = base.astype(BF16)
    core_copy().start()
    for which in range(N_EDGE):
        edge(I_MOM, moments, which).start()
    for copy in far_copies(0):
        copy.start()

    def prepare(slot):
        x = rows([pts[slot], jnp.zeros((5, PTS), F32)])
        padded[slot] = x
        packed, own_norm = features((x - x[:, 0:1]) * SCALE, True)
        feats[slot] = packed.T.astype(BF16)
        apart = (x[0:3] - pts[OWN][:, 0:1]) * SCALE
        apart_norm = jnp.sum(apart * apart, axis=0, keepdims=True) * FAR_SCALE
        norms[pl.ds(slot, 1)] = jnp.maximum(own_norm, apart_norm)

    def prepare_pair(i, carry):
        prepare(2 * i)
        prepare(2 * i + 1)
        return carry

    lax.fori_loop(OWN // 2, (OWN + LEAF) // 2, prepare_pair, 0)
    for which in range(N_EDGE):
        edge(I_PTS, pts, which).wait_recv()
    lax.fori_loop(0, OWN // 2, prepare_pair, 0)
    lax.fori_loop((OWN + LEAF) // 2, SLOTS // 2, prepare_pair, 0)

    def slot_of(entry):
        return jnp.clip(entry - me * LEAF + OWN, 0, SLOTS - 1)

    def build(leaf, column):
        slot = slot_of(near_list[leaf, column])
        target = (padded[OWN + leaf] - padded[slot][:, 0:1]) * SCALE
        packed, _ = features(target, False)
        squared = jnp.dot(feats[slot], packed.astype(BF16), preferred_element_type=F32)
        kernels[leaf * NEAR + column] = lax.rsqrt(
            jnp.maximum(squared, SOFT * SCALE * SCALE)
        ).astype(BF16)

    def core_step():
        core_copy().wait_recv()
        level[1] = (core_out[0] + core_in[0]).astype(BF16)
        line_out[...] = core_out[pl.ds(1, 2)] + core_in[pl.ds(1, 2)]
        for copy in line_copies():
            copy.start()
        window(2).start()
        window(3).start()
        for copy in far_copies(1):
            copy.start()

    def line_step():
        for copy in line_copies():
            copy.wait_recv()
        level[2] = (line_out[0] + line_in[0]).astype(BF16)
        third_level = (line_out[1] + line_in[1]) + (line_in[2] + line_in[3])
        level[3] = third_level.astype(BF16)
        column_own[...] = climb(1, third_level)
        column_out[...] = column_own[...].astype(BF16)
        for copy in column_copies():
            copy.start()
        for height in (2, 3):
            for copy in far_copies(height):
                copy.start()

    def column_step():
        for copy in column_copies():
            copy.wait_recv()
        for i in range(NEST):
            total = column_own[i]
            for k in range(1, 8):
                if column_first(k) <= i:
                    total += column_in[k - 1, i].astype(F32)
            level[NEST + 1 + i] = total.astype(BF16)
        for height in (6, 5, 4):
            for copy in far_copies(height):
                copy.start()

    def pass_step():
        window(1).wait_recv()
        window(4).start()

    def far_step(height):
        for copy in far_copies(height):
            copy.wait_recv()
        index = lax.div(me, 1 << height)
        total = devices >> height
        odd = lax.rem(index, 2)

        def kept(slot, usable):
            block = arrived[height, slot]
            return jnp.where(usable, block, jnp.zeros_like(block))

        last = 0 if height == LEVELS - 1 else 1
        stack = rows(
            [
                kept(2, (odd == 1) & (index >= 3)),
                kept(0, index >= 2),
                kept(last, index + 2 < total),
                kept(2, (odd == 0) & (index + 3 < total)),
            ]
        )
        far[pl.ds(height * RANK, RANK)] = jnp.dot(
            branch_c[height], stack, preferred_element_type=F32
        )

    def near_group(group, carry):
        leaf = lax.div(group, NEAR // GROUP)
        first = lax.rem(group, NEAR // GROUP) * GROUP
        for u in range(GROUP):
            build(leaf, first + u)
        for step, at in (
            (core_step, CORE_AT),
            (line_step, LINE_AT),
            (pass_step, PASS_AT),
            (column_step, COLUMN_AT),
        ):

            @pl.when(group == at)
            def _():
                step()

        for height, at in enumerate(FAR_AT):

            @pl.when(group == at)
            def _():
                if height == 0:
                    load_branch_c.wait()
                far_step(height)

        return carry

    lax.fori_loop(0, LEAF * NEAR // GROUP, near_group, 0)

    far_step(LEVELS - 1)
    upper = descend(1, far[pl.ds((NEST + 1) * RANK, NEST * RANK)])
    far[pl.ds(NEST * RANK, RANK)] += upper
    local = far[pl.ds(0, RANK)] + descend(0, far[pl.ds(RANK, NEST * RANK)])
    wide = jnp.concatenate(halves(local), axis=1)
    spread_both = lax.dot_general(
        transfer[...], wide, (((0,), (0,)), ((), ())), preferred_element_type=F32
    )
    spread[...] = (spread_both[:, :RHS] + spread_both[:, RHS:]).reshape(LEAF, RANK, RHS)
    load_coupling.wait()
    for which in range(N_EDGE):
        edge(I_MOM, moments, which).wait_recv()
    for which in (0, 2, 3, 4):
        window(which).wait_recv()
    keep = [
        pltpu.make_async_copy(charges, charges_out, store_sem.at[2]),
        pltpu.make_async_copy(pts, points_out, store_sem.at[3]),
        pltpu.make_async_copy(norms, norms_out, store_sem.at[4]),
    ]
    for copy in keep:
        copy.start()

    def out_copy(leaf, buf):
        return pltpu.make_async_copy(
            out_buf.at[buf], field.at[:, pl.ds(pl.multiple_of(leaf * PTS, PTS), PTS)], store_sem.at[buf]
        )

    def finish(leaf, buf):
        blocks = []
        for j in range(FAR):
            block = moments[slot_of(far_list[j, leaf])]
            blocks.append(jnp.where(j < far_count[leaf], block.astype(F32), 0.0).astype(BF16))
        here = jnp.dot(coupling[leaf], rows(blocks), preferred_element_type=F32) + spread[leaf]
        here = here.astype(BF16)
        leaf_local[leaf] = here
        total = lax.dot_general(
            here, basis[leaf], (((0,), (0,)), ((), ())), preferred_element_type=F32
        )
        for j in range(NEAR):
            block = charges[slot_of(near_list[leaf, j])]
            block = jnp.where(j < near_count[leaf], block, jnp.zeros_like(block))
            total += jnp.dot(block, kernels[leaf * NEAR + j], preferred_element_type=F32)
        out_buf[buf] = total
        out_copy(leaf, buf).start()

    def finish_pair(i, carry):
        for buf in range(2):

            @pl.when(i > 0)
            def _():
                out_copy(2 * i - 2 + buf, buf).wait()

            finish(2 * i + buf, buf)
        return carry

    lax.fori_loop(0, LEAF // 2, finish_pair, 0)
    out_copy(LEAF - 2, 0).wait()
    out_copy(LEAF - 1, 1).wait()
    keep.append(pltpu.make_async_copy(leaf_local, leaf_local_out, store_sem.at[5]))
    keep[-1].start()
    for copy in keep:
        copy.wait()
    for which in range(N_EDGE):
        edge(I_PTS, pts, which).wait_send()
        edge(I_MOM, moments, which).wait_send()
    for which in range(5):
        window(which).wait_send()
    for copy in [core_copy()] + line_copies() + column_copies():
        copy.wait_send()
    for height in range(LEVELS):
        for copy in far_copies(height):
            copy.wait_send()


N_LOAD = 2 * LEAF + 5


def tree(devices, *operands):
    any_spec = pl.BlockSpec(memory_space=pl.ANY)
    smem_spec = pl.BlockSpec(memory_space=pltpu.SMEM)
    return pl.pallas_call(
        functools.partial(tree_kernel, devices),
        out_shape=(
            jax.ShapeDtypeStruct((RHS, LEAF * PTS), F32),
            jax.ShapeDtypeStruct((LEAF, RANK, RHS), BF16),
            jax.ShapeDtypeStruct((SLOTS, PTS), F32),
            jax.ShapeDtypeStruct((SLOTS, RHS, PTS), BF16),
            jax.ShapeDtypeStruct((SLOTS, 3, PTS), F32),
        ),
        in_specs=[smem_spec] * 4 + [any_spec] * 7,
        out_specs=(any_spec,) * 5,
        scratch_shapes=[
            pltpu.VMEM((SLOTS, RHS, PTS), BF16),
            pltpu.VMEM((SLOTS, 3, PTS), F32),
            pltpu.VMEM((SLOTS, RANK, RHS), BF16),
            pltpu.VMEM((SLOTS, PTS, FEAT), BF16),
            pltpu.VMEM((SLOTS, 8, PTS), F32),
            pltpu.VMEM((LEAF * NEAR, PTS, PTS), BF16),
            pltpu.VMEM((LEAF, RANK, PTS), BF16),
            pltpu.VMEM((RANK, LEAF * RANK), BF16),
            pltpu.VMEM((LEAF, RANK, FAR * RANK), BF16),
            pltpu.VMEM((UP, RANK, 2 * RANK), BF16),
            pltpu.VMEM((LEVELS, RANK, 4 * RANK), BF16),
            pltpu.VMEM((2, NEST * RANK, 2 * RANK), BF16),
            pltpu.VMEM((LEVELS, RANK, RHS), BF16),
            pltpu.VMEM((NEST, RANK, RHS), F32),
            pltpu.VMEM((NEST, RANK, RHS), F32),
            pltpu.VMEM((2, RANK, RHS), F32),
            pltpu.VMEM((4, RANK, RHS), F32),
            pltpu.VMEM((NEST, RANK, RHS), F32),
            pltpu.VMEM((NEST, RANK, RHS), BF16),
            pltpu.VMEM((7, NEST, RANK, RHS), BF16),
            pltpu.VMEM((LEVELS, 3, RANK, RHS), BF16),
            pltpu.VMEM((LEVELS * RANK, RHS), F32),
            pltpu.VMEM((LEAF, RANK, RHS), F32),
            pltpu.VMEM((SLOTS, PTS), F32),
            pltpu.VMEM((LEAF, RANK, RHS), BF16),
            pltpu.VMEM((2, RHS, PTS), F32),
            pltpu.SemaphoreType.DMA((N_LOAD,)),
            pltpu.SemaphoreType.DMA((6,)),
            pltpu.SemaphoreType.DMA((N_MSG,)),
            pltpu.SemaphoreType.DMA((N_MSG,)),
        ],
        compiler_params=pltpu.CompilerParams(
            collective_id=0, has_side_effects=True, vmem_limit_bytes=66_000_000
        ),
        name="tree",
    )(*operands)


def result_kernel(
    near_list, near_count, norms, fast, leaf_local, charges, points, basis, field,
    buf, charge_buf, point_buf, local_buf, basis_buf, norm_buf, in_sem, out_sem, sem,
):
    def cols(leaf):
        return pl.ds(leaf * PTS, PTS)

    reads = [
        pltpu.make_async_copy(fast.at[:, cols(i)], buf.at[i], in_sem.at[i]) for i in range(LEAF)
    ]
    writes = [
        pltpu.make_async_copy(buf.at[i], field.at[:, cols(i)], out_sem.at[i]) for i in range(LEAF)
    ]
    get_norms = pltpu.make_async_copy(norms, norm_buf, sem)
    get_norms.start()
    for copy in reads:
        copy.start()
    get_norms.wait()
    direct = jnp.max(jnp.where(norm_buf[...] <= EXTENT, 0.0, 1.0)) > 0.0

    @pl.when(jnp.logical_not(direct))
    def _():
        for read, write in zip(reads, writes):
            read.wait()
            write.start()
        for write in writes:
            write.wait()

    @pl.when(direct)
    def _():
        me = lax.axis_index("box")
        for read in reads:
            read.wait()

        def fetch(src, dst):
            copy = pltpu.make_async_copy(src, dst, sem)
            copy.start()
            copy.wait()

        fetch(points, point_buf)
        fetch(leaf_local, local_buf)
        fetch(basis, basis_buf)

        def one(leaf, carry):
            buf[0] = lax.dot_general(
                local_buf[leaf], basis_buf[leaf], (((0,), (0,)), ((), ())), preferred_element_type=F32
            )
            target = point_buf[OWN + leaf]

            def pair(j, inner):
                slot = jnp.clip(near_list[leaf, j] - me * LEAF + OWN, 0, SLOTS - 1)
                fetch(charges.at[slot], charge_buf)
                column = point_buf[slot].T
                squared = SOFT
                for axis in range(3):
                    gap = column[:, axis : axis + 1] - target[axis : axis + 1]
                    squared = squared + gap * gap
                block = (INV * lax.rsqrt(squared)).astype(BF16)
                buf[0] += jnp.dot(charge_buf[...], block, preferred_element_type=F32)
                return inner

            lax.fori_loop(0, near_count[leaf], pair, 0)
            fetch(buf.at[0], field.at[:, pl.ds(pl.multiple_of(leaf * PTS, PTS), PTS)])
            return carry

        lax.fori_loop(0, LEAF, one, 0)


def result(*operands):
    any_spec = pl.BlockSpec(memory_space=pl.ANY)
    smem_spec = pl.BlockSpec(memory_space=pltpu.SMEM)
    return pl.pallas_call(
        result_kernel,
        out_shape=jax.ShapeDtypeStruct((RHS, LEAF * PTS), F32),
        in_specs=[smem_spec] * 2 + [any_spec] * 6,
        out_specs=any_spec,
        scratch_shapes=[
            pltpu.VMEM((LEAF, RHS, PTS), F32),
            pltpu.VMEM((RHS, PTS), BF16),
            pltpu.VMEM((SLOTS, 3, PTS), F32),
            pltpu.VMEM((LEAF, RANK, RHS), BF16),
            pltpu.VMEM((LEAF, RANK, PTS), BF16),
            pltpu.VMEM((SLOTS, PTS), F32),
            pltpu.SemaphoreType.DMA((LEAF,)),
            pltpu.SemaphoreType.DMA((LEAF,)),
            pltpu.SemaphoreType.DMA,
        ],
        name="result",
    )(*operands)


def on_device(
    sources, points, near_list, near_count, far_list, far_count,
    leaf_basis, leaf_transfer, leaf_coupling, branch_transfer, branch_coupling,
):
    devices = lax.axis_size("box")
    fast, leaf_local, norms, charges, window_points = tree(
        devices, near_list, near_count, far_list.T, far_count, sources, points,
        leaf_basis, leaf_transfer, leaf_coupling, branch_transfer, branch_coupling,
    )
    return result(
        near_list, near_count, norms, fast, leaf_local, charges, window_points, leaf_basis
    )


def solution(mesh):
    placed = (
        P(None, "box"),
        P(None, "box"),
        P("box", None),
        P("box"),
        P("box", None),
        P("box"),
        P("box", None, None),
        P("box", None, None),
        P("box", None, None),
        P("box", None, None, None),
        P("box", None, None, None),
    )
    return jax.shard_map(
        on_device, mesh=mesh, in_specs=placed, out_specs=P(None, "box"), check_vma=False
    )
```

```python
import functools

import jax
import jax.numpy as jnp
from jax import lax
from jax.experimental import pallas as pl
from jax.experimental.pallas import tpu as pltpu
from jax.sharding import PartitionSpec as P

F32 = jnp.float32
BF16 = jnp.bfloat16
SOFT = 0.25
INV = 0.07957747154594767
SCALE = 1.0 / INV
EXTENT = 1024.0 * SCALE * SCALE
FAR_SCALE = 1e-27
LEAF = 8
PTS = 512
RANK = 64
RHS = 128
NEAR = 12
FAR = 4
REACH = 12
SLOTS = LEAF + 2 * REACH
OWN = REACH
UP = 6
LEVELS = 7
FEAT = 48
GROUP = 6
MESH = pl.DeviceIdType.MESH

EDGES = ((1, 0, 8), (-1, 0, 8), (2, 4, 4), (-2, 0, 4))
N_EDGE = len(EDGES)
NEST = 3
PAIR = (6, 24, 40, 48, 56)
I_PTS = 0
I_MOM = I_PTS + N_EDGE
I_WIN = I_MOM + N_EDGE
N_WIN = 14
I_CORE = I_WIN + N_WIN
I_LINE = I_CORE + 1
I_COLUMN = I_LINE + 3
I_FAR = I_COLUMN + 7
N_MSG = I_FAR + 3 * LEVELS

LINE_AT, PASS_AT, COLUMN_AT, MOMENTS_AT, DOWN_AT = 0, 4, 5, 8, 15
FAR_AT = (6, 7, 10, 8, 11, 12, 13)
CHARGES_FROM, CHARGES_TO = 0, 8


def split3(x):
    a = x.astype(BF16)
    r = x - a.astype(F32)
    b = r.astype(BF16)
    return a, b, (r - b.astype(F32)).astype(BF16)


def rows(parts):
    return jnp.concatenate(parts, axis=0)


def halves(x):
    high = x.astype(BF16)
    return high, (x - high.astype(F32)).astype(BF16)


def features(x, of_source):
    row = lax.broadcasted_iota(jnp.int32, x.shape, 0)
    n = jnp.sum(x * x, axis=0, keepdims=True)
    a, b, c = (v.astype(F32) for v in split3(x if of_source else -2.0 * x))
    n0, n1, n2 = (v.astype(F32) for v in split3(n + SOFT * SCALE * SCALE if of_source else n))
    norm = jnp.where(row == 3, n0, jnp.where(row == 4, n1, jnp.where(row == 5, n2, 0.0)))
    ones = jnp.where((row >= 3) & (row < 6), 1.0, 0.0)
    if of_source:
        parts = [a + norm, b + ones, a, b, c, a]
    else:
        parts = [a + ones, a + norm, b, b, a, c]
    return rows(parts), n


def exact_dot(left, right):
    width = right.shape[1]
    both = jnp.dot(left, jnp.concatenate(halves(right), axis=1), preferred_element_type=F32)
    return both[:, :width] + both[:, width:]


def tree_kernel(
    devices,
    near_list,
    near_count,
    far_list,
    far_count,
    sources,
    points,
    basis_in,
    leaf_transfer_in,
    coupling_in,
    branch_transfer_in,
    branch_coupling_in,
    field,
    leaf_local_out,
    norms_out,
    charges_out,
    points_out,
    charges,
    pts,
    moments,
    feats,
    padded,
    kernels,
    basis,
    transfer,
    coupling,
    branch_t,
    branch_c,
    ladder,
    level,
    core_out,
    core_in,
    line_out,
    line_in,
    column_own,
    column_out,
    column_in,
    arrived,
    far,
    spread,
    norms,
    leaf_local,
    out_buf,
    load_sem,
    store_sem,
    send_sem,
    recv_sem,
):
    me = lax.axis_index("box")

    def other(distance):
        return lax.rem(me + distance + devices, devices)

    def flipped(pattern):
        return lax.bitwise_xor(me, pattern)

    odd_core = lax.rem(me, 2)
    sibling = me + 1 - 2 * odd_core

    def third(height):
        odd = lax.rem(lax.div(me, 1 << height), 2)
        return other((3 - 6 * odd) * (1 << height))

    def remote(index, src, dst, device):
        return pltpu.make_async_remote_copy(
            src_ref=src,
            dst_ref=dst,
            send_sem=send_sem.at[index],
            recv_sem=recv_sem.at[index],
            device_id=(device,),
            device_id_type=MESH,
        )

    barrier = pltpu.get_barrier_semaphore()
    partners = [other(s * (1 << k)) for k in range(LEVELS) for s in (1, -1)]
    partners += [other(devices // 2)] + [third(h) for h in range(LEVELS)]
    partners += [flipped(pattern) for pattern in PAIR]
    for partner in partners:
        pl.semaphore_signal(barrier, inc=1, device_id=(partner,), device_id_type=MESH)

    loads = []

    def load(src, dst):
        copy = pltpu.make_async_copy(src, dst, load_sem.at[len(loads)])
        copy.start()
        loads.append(copy)
        return copy

    load_points = [load(points.at[:, pl.ds(i * PTS, PTS)], pts.at[OWN + i]) for i in range(LEAF)]
    load_charges = [
        load(sources.at[:, pl.ds(i * PTS, PTS)], charges.at[OWN + i]) for i in range(LEAF)
    ]
    load_basis = load(basis_in, basis)
    load_transfer = load(leaf_transfer_in.at[0], transfer)
    load_branch_t = load(branch_transfer_in.at[0], branch_t)
    load_branch_c = load(branch_coupling_in.at[0], branch_c)
    load_coupling = load(coupling_in, coupling)

    def edge(base, buf, which):
        distance, first, count = EDGES[which]
        return remote(
            base + which,
            buf.at[pl.ds(OWN + first, count)],
            buf.at[pl.ds(OWN + first - LEAF * distance, count)],
            other(distance),
        )

    def window(which):
        if which == 0:
            return remote(
                I_WIN,
                charges.at[pl.ds(OWN, LEAF)],
                charges.at[pl.ds(4 + 16 * odd_core, LEAF)],
                sibling,
            )
        first, there = 8 + 12 * odd_core, 28 * odd_core
        return remote(
            I_WIN + 1, charges.at[pl.ds(first, 4)], charges.at[pl.ds(there, 4)], sibling
        )

    def ahead(k):
        leaf = lax.rem(k + 4 * odd_core, LEAF)
        return remote(
            I_WIN + 2 + k,
            charges.at[pl.ds(OWN + leaf, 1)],
            charges.at[pl.ds(leaf + 20 - 16 * odd_core, 1)],
            other(2 * odd_core - 1),
        )

    def behind(k):
        return remote(
            I_WIN + 10 + k,
            charges.at[pl.ds(OWN + 4 - 4 * odd_core + k, 1)],
            charges.at[pl.ds(28 * odd_core + k, 1)],
            other(2 - 4 * odd_core),
        )

    def core_copy():
        return remote(I_CORE, core_out, core_in, sibling)

    def line_copies():
        return [
            remote(I_LINE, line_out, line_in.at[pl.ds(0, 2)], flipped(2)),
            remote(I_LINE + 1, line_out.at[1], line_in.at[2], flipped(4)),
            remote(I_LINE + 2, line_out.at[1], line_in.at[3], flipped(6)),
        ]

    def column_first(k):
        return 0 if k == 1 else 1 if k < 4 else 2

    def column_copies():
        copies = []
        for k in range(1, 8):
            part = pl.ds(column_first(k), NEST - column_first(k))
            copies.append(
                remote(
                    I_COLUMN + k - 1, column_out.at[part], column_in.at[k - 1, part], flipped(8 * k)
                )
            )
        return copies

    def far_copies(height):
        step = 1 << height
        copies = []
        for slot, device in ((0, other(2 * step)), (1, other(-2 * step)), (2, third(height))):
            if height == LEVELS - 1 and slot == 1:
                continue
            copies.append(
                remote(I_FAR + 3 * height + slot, level.at[height], arrived.at[height, slot], device)
            )
        return copies

    def half(height):
        bit = lax.rem(lax.div(me, 1 << height), 2)
        joined = branch_t[height].astype(F32)
        return jnp.where(bit == 1, joined[:, RANK:], joined[:, :RANK]).astype(BF16)

    for copy in load_points:
        copy.wait()
    pl.semaphore_wait(barrier, len(partners))
    for which in range(N_EDGE):
        edge(I_PTS, pts, which).start()
    for copy in load_charges:
        copy.wait()
    ahead(0).start()
    ahead(1).start()
    window(0).start()

    load_basis.wait()
    load_transfer.wait()
    load_branch_t.wait()
    for i in range(LEAF):
        moments[OWN + i] = lax.dot_general(
            basis[i], charges[OWN + i], (((1,), (1,)), ((), ())), preferred_element_type=F32
        ).astype(BF16)
    base = jnp.dot(
        transfer[...],
        moments[pl.ds(OWN, LEAF)].reshape(LEAF * RANK, RHS),
        preferred_element_type=F32,
    )
    for nest in range(2):
        first, second, last = (half(NEST * nest + i) for i in range(NEST))
        two = jnp.dot(second, first, preferred_element_type=F32)
        three = exact_dot(last, two)
        high, low = halves(rows([first.astype(F32), two, three]))
        ladder[nest] = jnp.concatenate([high, low], axis=1)

    def climb(nest, x):
        high, low = halves(x)
        pair = ladder[nest]
        wide = jnp.concatenate([high, low], axis=1)
        r = jnp.dot(pair[:, :RANK], wide, preferred_element_type=F32)
        fine = jnp.dot(pair[:, RANK:], high, preferred_element_type=F32)
        return (r[:, :RHS] + r[:, RHS:] + fine).reshape(NEST, RANK, RHS)

    def descend(nest, x):
        wide = jnp.concatenate(halves(x), axis=1)
        r = lax.dot_general(
            ladder[nest], wide, (((0,), (0,)), ((), ())), preferred_element_type=F32
        )
        return r[:RANK, :RHS] + r[:RANK, RHS:] + r[RANK:, :RHS]

    core_out[...] = climb(0, base)
    level[0] = base.astype(BF16)
    core_copy().start()
    ahead(2).start()
    ahead(3).start()

    def core_step():
        core_copy().wait_recv()
        level[1] = (core_out[0] + core_in[0]).astype(BF16)
        line_out[...] = core_out[pl.ds(1, 2)] + core_in[pl.ds(1, 2)]
        for copy in line_copies():
            copy.start()

    def prepare(slot):
        x = rows([pts[slot], jnp.zeros((5, PTS), F32)])
        padded[slot] = x
        packed, own_norm = features((x - x[:, 0:1]) * SCALE, True)
        feats[slot] = packed.T.astype(BF16)
        apart = (x[0:3] - pts[OWN][:, 0:1]) * SCALE
        apart_norm = jnp.sum(apart * apart, axis=0, keepdims=True) * FAR_SCALE
        norms[pl.ds(slot, 1)] = jnp.maximum(own_norm, apart_norm)

    def prepare_pair(i, carry):
        prepare(2 * i)
        prepare(2 * i + 1)
        return carry

    lax.fori_loop(OWN // 2, (OWN + LEAF) // 2, prepare_pair, 0)
    core_step()
    for which in range(N_EDGE):
        edge(I_PTS, pts, which).wait_recv()
    lax.fori_loop(0, OWN // 2, prepare_pair, 0)
    lax.fori_loop((OWN + LEAF) // 2, SLOTS // 2, prepare_pair, 0)

    def slot_of(entry):
        return jnp.clip(entry - me * LEAF + OWN, 0, SLOTS - 1)

    def build(leaf, column):
        slot = slot_of(near_list[leaf, column])
        target = (padded[OWN + leaf] - padded[slot][:, 0:1]) * SCALE
        packed, _ = features(target, False)
        squared = jnp.dot(feats[slot], packed.astype(BF16), preferred_element_type=F32)
        kernels[leaf * NEAR + column] = lax.rsqrt(
            jnp.maximum(squared, SOFT * SCALE * SCALE)
        ).astype(BF16)

    def line_step():
        for copy in line_copies():
            copy.wait_recv()
        level[2] = (line_out[0] + line_in[0]).astype(BF16)
        third_level = (line_out[1] + line_in[1]) + (line_in[2] + line_in[3])
        level[3] = third_level.astype(BF16)
        column_own[...] = climb(1, third_level)
        column_out[...] = column_own[...].astype(BF16)
        for copy in column_copies():
            copy.start()
        for height in (3, 2, 1, 0):
            for copy in far_copies(height):
                copy.start()

    def column_step():
        for copy in column_copies():
            copy.wait_recv()
        for i in range(NEST):
            total = column_own[i]
            for k in range(1, 8):
                if column_first(k) <= i:
                    total += column_in[k - 1, i].astype(F32)
            level[NEST + 1 + i] = total.astype(BF16)
        for height in (6, 5, 4):
            for copy in far_copies(height):
                copy.start()

    def pass_step():
        for k in range(4):
            ahead(k).wait_recv()
        window(1).start()

    def moments_step():
        for which in range(N_EDGE):
            edge(I_MOM, moments, which).start()

    def far_step(height):
        for copy in far_copies(height):
            copy.wait_recv()
        index = lax.div(me, 1 << height)
        total = devices >> height
        odd = lax.rem(index, 2)

        def kept(slot, usable):
            block = arrived[height, slot]
            return jnp.where(usable, block, jnp.zeros_like(block))

        last = 0 if height == LEVELS - 1 else 1
        stack = rows(
            [
                kept(2, (odd == 1) & (index >= 3)),
                kept(0, index >= 2),
                kept(last, index + 2 < total),
                kept(2, (odd == 0) & (index + 3 < total)),
            ]
        )
        far[pl.ds(height * RANK, RANK)] = jnp.dot(
            branch_c[height], stack, preferred_element_type=F32
        )

    def down_step():
        upper = descend(1, far[pl.ds((NEST + 1) * RANK, NEST * RANK)])
        far[pl.ds(NEST * RANK, RANK)] += upper
        local = far[pl.ds(0, RANK)] + descend(0, far[pl.ds(RANK, NEST * RANK)])
        wide = jnp.concatenate(halves(local), axis=1)
        spread_both = lax.dot_general(
            transfer[...], wide, (((0,), (0,)), ((), ())), preferred_element_type=F32
        )
        spread[...] = (spread_both[:, :RHS] + spread_both[:, RHS:]).reshape(LEAF, RANK, RHS)

    def near_group(group, carry):
        leaf = lax.div(group, NEAR // GROUP)
        first = lax.rem(group, NEAR // GROUP) * GROUP
        for u in range(GROUP):
            build(leaf, first + u)
        @pl.when((group >= CHARGES_FROM) & (group < CHARGES_FROM + 4))
        def _():
            ahead(4 + group - CHARGES_FROM).start()

        @pl.when((group >= CHARGES_FROM + 4) & (group < CHARGES_TO))
        def _():
            behind(group - CHARGES_FROM - 4).start()

        for step, at in (
            (line_step, LINE_AT),
            (pass_step, PASS_AT),
            (column_step, COLUMN_AT),
            (moments_step, MOMENTS_AT),
            (down_step, DOWN_AT),
        ):

            @pl.when(group == at)
            def _():
                step()

        for height, at in enumerate(FAR_AT):

            @pl.when(group == at)
            def _():
                if height == 0:
                    load_branch_c.wait()
                far_step(height)

        return carry

    lax.fori_loop(0, LEAF * NEAR // GROUP, near_group, 0)

    load_coupling.wait()
    for which in range(N_EDGE):
        edge(I_MOM, moments, which).wait_recv()
    window(0).wait_recv()
    window(1).wait_recv()
    for k in range(4):
        ahead(4 + k).wait_recv()
        behind(k).wait_recv()
    keep = [
        pltpu.make_async_copy(charges, charges_out, store_sem.at[2]),
        pltpu.make_async_copy(pts, points_out, store_sem.at[3]),
        pltpu.make_async_copy(norms, norms_out, store_sem.at[4]),
    ]
    for copy in keep:
        copy.start()

    def out_copy(leaf, buf):
        return pltpu.make_async_copy(
            out_buf.at[buf], field.at[:, pl.ds(pl.multiple_of(leaf * PTS, PTS), PTS)], store_sem.at[buf]
        )

    def finish(leaf, buf):
        blocks = []
        for j in range(FAR):
            block = moments[slot_of(far_list[j, leaf])]
            blocks.append(jnp.where(j < far_count[leaf], block.astype(F32), 0.0).astype(BF16))
        here = jnp.dot(coupling[leaf], rows(blocks), preferred_element_type=F32) + spread[leaf]
        here = here.astype(BF16)
        leaf_local[leaf] = here
        total = lax.dot_general(
            here, basis[leaf], (((0,), (0,)), ((), ())), preferred_element_type=F32
        )
        for j in range(NEAR):
            block = charges[slot_of(near_list[leaf, j])]
            block = jnp.where(j < near_count[leaf], block, jnp.zeros_like(block))
            total += jnp.dot(block, kernels[leaf * NEAR + j], preferred_element_type=F32)
        out_buf[buf] = total
        out_copy(leaf, buf).start()

    def finish_pair(i, carry):
        for buf in range(2):

            @pl.when(i > 0)
            def _():
                out_copy(2 * i - 2 + buf, buf).wait()

            finish(2 * i + buf, buf)
        return carry

    lax.fori_loop(0, LEAF // 2, finish_pair, 0)
    out_copy(LEAF - 2, 0).wait()
    out_copy(LEAF - 1, 1).wait()
    keep.append(pltpu.make_async_copy(leaf_local, leaf_local_out, store_sem.at[5]))
    keep[-1].start()
    for copy in keep:
        copy.wait()
    for which in range(N_EDGE):
        edge(I_PTS, pts, which).wait_send()
        edge(I_MOM, moments, which).wait_send()
    window(0).wait_send()
    window(1).wait_send()
    for k in range(8):
        ahead(k).wait_send()
    for k in range(4):
        behind(k).wait_send()
    for copy in [core_copy()] + line_copies() + column_copies():
        copy.wait_send()
    for height in range(LEVELS):
        for copy in far_copies(height):
            copy.wait_send()


N_LOAD = 2 * LEAF + 5


def tree(devices, *operands):
    any_spec = pl.BlockSpec(memory_space=pl.ANY)
    smem_spec = pl.BlockSpec(memory_space=pltpu.SMEM)
    return pl.pallas_call(
        functools.partial(tree_kernel, devices),
        out_shape=(
            jax.ShapeDtypeStruct((RHS, LEAF * PTS), F32),
            jax.ShapeDtypeStruct((LEAF, RANK, RHS), BF16),
            jax.ShapeDtypeStruct((SLOTS, PTS), F32),
            jax.ShapeDtypeStruct((SLOTS, RHS, PTS), BF16),
            jax.ShapeDtypeStruct((SLOTS, 3, PTS), F32),
        ),
        in_specs=[smem_spec] * 4 + [any_spec] * 7,
        out_specs=(any_spec,) * 5,
        scratch_shapes=[
            pltpu.VMEM((SLOTS, RHS, PTS), BF16),
            pltpu.VMEM((SLOTS, 3, PTS), F32),
            pltpu.VMEM((SLOTS, RANK, RHS), BF16),
            pltpu.VMEM((SLOTS, PTS, FEAT), BF16),
            pltpu.VMEM((SLOTS, 8, PTS), F32),
            pltpu.VMEM((LEAF * NEAR, PTS, PTS), BF16),
            pltpu.VMEM((LEAF, RANK, PTS), BF16),
            pltpu.VMEM((RANK, LEAF * RANK), BF16),
            pltpu.VMEM((LEAF, RANK, FAR * RANK), BF16),
            pltpu.VMEM((UP, RANK, 2 * RANK), BF16),
            pltpu.VMEM((LEVELS, RANK, 4 * RANK), BF16),
            pltpu.VMEM((2, NEST * RANK, 2 * RANK), BF16),
            pltpu.VMEM((LEVELS, RANK, RHS), BF16),
            pltpu.VMEM((NEST, RANK, RHS), F32),
            pltpu.VMEM((NEST, RANK, RHS), F32),
            pltpu.VMEM((2, RANK, RHS), F32),
            pltpu.VMEM((4, RANK, RHS), F32),
            pltpu.VMEM((NEST, RANK, RHS), F32),
            pltpu.VMEM((NEST, RANK, RHS), BF16),
            pltpu.VMEM((7, NEST, RANK, RHS), BF16),
            pltpu.VMEM((LEVELS, 3, RANK, RHS), BF16),
            pltpu.VMEM((LEVELS * RANK, RHS), F32),
            pltpu.VMEM((LEAF, RANK, RHS), F32),
            pltpu.VMEM((SLOTS, PTS), F32),
            pltpu.VMEM((LEAF, RANK, RHS), BF16),
            pltpu.VMEM((2, RHS, PTS), F32),
            pltpu.SemaphoreType.DMA((N_LOAD,)),
            pltpu.SemaphoreType.DMA((6,)),
            pltpu.SemaphoreType.DMA((N_MSG,)),
            pltpu.SemaphoreType.DMA((N_MSG,)),
        ],
        compiler_params=pltpu.CompilerParams(
            collective_id=0, has_side_effects=True, vmem_limit_bytes=66_000_000
        ),
        name="tree",
    )(*operands)


def result_kernel(
    near_list, near_count, norms, fast, leaf_local, charges, points, basis, field,
    buf, charge_buf, point_buf, local_buf, basis_buf, norm_buf, in_sem, out_sem, sem,
):
    def cols(leaf):
        return pl.ds(leaf * PTS, PTS)

    reads = [
        pltpu.make_async_copy(fast.at[:, cols(i)], buf.at[i], in_sem.at[i]) for i in range(LEAF)
    ]
    writes = [
        pltpu.make_async_copy(buf.at[i], field.at[:, cols(i)], out_sem.at[i]) for i in range(LEAF)
    ]
    get_norms = pltpu.make_async_copy(norms, norm_buf, sem)
    get_norms.start()
    for copy in reads:
        copy.start()
    get_norms.wait()
    direct = jnp.max(jnp.where(norm_buf[...] <= EXTENT, 0.0, 1.0)) > 0.0

    @pl.when(jnp.logical_not(direct))
    def _():
        for read, write in zip(reads, writes):
            read.wait()
            write.start()
        for write in writes:
            write.wait()

    @pl.when(direct)
    def _():
        me = lax.axis_index("box")
        for read in reads:
            read.wait()

        def fetch(src, dst):
            copy = pltpu.make_async_copy(src, dst, sem)
            copy.start()
            copy.wait()

        fetch(points, point_buf)
        fetch(leaf_local, local_buf)
        fetch(basis, basis_buf)

        def one(leaf, carry):
            buf[0] = lax.dot_general(
                local_buf[leaf], basis_buf[leaf], (((0,), (0,)), ((), ())), preferred_element_type=F32
            )
            target = point_buf[OWN + leaf]

            def pair(j, inner):
                slot = jnp.clip(near_list[leaf, j] - me * LEAF + OWN, 0, SLOTS - 1)
                fetch(charges.at[slot], charge_buf)
                column = point_buf[slot].T
                squared = SOFT
                for axis in range(3):
                    gap = column[:, axis : axis + 1] - target[axis : axis + 1]
                    squared = squared + gap * gap
                block = (INV * lax.rsqrt(squared)).astype(BF16)
                buf[0] += jnp.dot(charge_buf[...], block, preferred_element_type=F32)
                return inner

            lax.fori_loop(0, near_count[leaf], pair, 0)
            fetch(buf.at[0], field.at[:, pl.ds(pl.multiple_of(leaf * PTS, PTS), PTS)])
            return carry

        lax.fori_loop(0, LEAF, one, 0)


def result(*operands):
    any_spec = pl.BlockSpec(memory_space=pl.ANY)
    smem_spec = pl.BlockSpec(memory_space=pltpu.SMEM)
    return pl.pallas_call(
        result_kernel,
        out_shape=jax.ShapeDtypeStruct((RHS, LEAF * PTS), F32),
        in_specs=[smem_spec] * 2 + [any_spec] * 6,
        out_specs=any_spec,
        scratch_shapes=[
            pltpu.VMEM((LEAF, RHS, PTS), F32),
            pltpu.VMEM((RHS, PTS), BF16),
            pltpu.VMEM((SLOTS, 3, PTS), F32),
            pltpu.VMEM((LEAF, RANK, RHS), BF16),
            pltpu.VMEM((LEAF, RANK, PTS), BF16),
            pltpu.VMEM((SLOTS, PTS), F32),
            pltpu.SemaphoreType.DMA((LEAF,)),
            pltpu.SemaphoreType.DMA((LEAF,)),
            pltpu.SemaphoreType.DMA,
        ],
        name="result",
    )(*operands)


def on_device(
    sources, points, near_list, near_count, far_list, far_count,
    leaf_basis, leaf_transfer, leaf_coupling, branch_transfer, branch_coupling,
):
    devices = lax.axis_size("box")
    fast, leaf_local, norms, charges, window_points = tree(
        devices, near_list, near_count, far_list.T, far_count, sources, points,
        leaf_basis, leaf_transfer, leaf_coupling, branch_transfer, branch_coupling,
    )
    return result(
        near_list, near_count, norms, fast, leaf_local, charges, window_points, leaf_basis
    )


def solution(mesh):
    placed = (
        P(None, "box"),
        P(None, "box"),
        P("box", None),
        P("box"),
        P("box", None),
        P("box"),
        P("box", None, None),
        P("box", None, None),
        P("box", None, None),
        P("box", None, None, None),
        P("box", None, None, None),
    )
    return jax.shard_map(
        on_device, mesh=mesh, in_specs=placed, out_specs=P(None, "box"), check_vma=False
    )
```

```python
import functools

import jax
import jax.numpy as jnp
from jax import lax
from jax.experimental import pallas as pl
from jax.experimental.pallas import tpu as pltpu
from jax.sharding import PartitionSpec as P

F32 = jnp.float32
BF16 = jnp.bfloat16
SOFT = 0.25
INV = 0.07957747154594767
SCALE = 1.0 / INV
EXTENT = 1024.0 * SCALE * SCALE
FAR_SCALE = 1e-27
LEAF = 8
PTS = 512
RANK = 64
RHS = 128
NEAR = 12
FAR = 4
REACH = 12
SLOTS = LEAF + 2 * REACH
OWN = REACH
UP = 6
LEVELS = 7
FEAT = 48
GROUP = 12
MESH = pl.DeviceIdType.MESH

EDGES = ((1, 0, 8), (-1, 0, 8), (2, 4, 4), (-2, 0, 4))
N_EDGE = len(EDGES)
NEST = 3
PAIR = (6, 24, 40, 48, 56)
I_PTS = 0
I_MOM = I_PTS + N_EDGE
I_WIN = I_MOM + N_EDGE
N_WIN = 14
I_CORE = I_WIN + N_WIN
I_LINE = I_CORE + 1
I_COLUMN = I_LINE + 3
I_FAR = I_COLUMN + 7
N_MSG = I_FAR + 3 * LEVELS

LINE_AT, PASS_AT, COLUMN_AT, MOMENTS_AT, DOWN_AT = 0, 2, 2, 5, 7
FAR_AT = (3, 3, 5, 4, 5, 6, 6)


def split3(x):
    a = x.astype(BF16)
    r = x - a.astype(F32)
    b = r.astype(BF16)
    return a, b, (r - b.astype(F32)).astype(BF16)


def rows(parts):
    return jnp.concatenate(parts, axis=0)


def halves(x):
    high = x.astype(BF16)
    return high, (x - high.astype(F32)).astype(BF16)


def features(x, of_source):
    row = lax.broadcasted_iota(jnp.int32, x.shape, 0)
    n = jnp.sum(x * x, axis=0, keepdims=True)
    a, b, c = (v.astype(F32) for v in split3(x if of_source else -2.0 * x))
    n0, n1, n2 = (v.astype(F32) for v in split3(n + SOFT * SCALE * SCALE if of_source else n))
    norm = jnp.where(row == 3, n0, jnp.where(row == 4, n1, jnp.where(row == 5, n2, 0.0)))
    ones = jnp.where((row >= 3) & (row < 6), 1.0, 0.0)
    if of_source:
        parts = [a + norm, b + ones, a, b, c, a]
    else:
        parts = [a + ones, a + norm, b, b, a, c]
    return rows(parts), n


def exact_dot(left, right):
    width = right.shape[1]
    both = jnp.dot(left, jnp.concatenate(halves(right), axis=1), preferred_element_type=F32)
    return both[:, :width] + both[:, width:]


def tree_kernel(
    devices,
    near_list,
    near_count,
    far_list,
    far_count,
    sources,
    points,
    basis_in,
    leaf_transfer_in,
    coupling_in,
    branch_transfer_in,
    branch_coupling_in,
    field,
    leaf_local_out,
    norms_out,
    charges_out,
    points_out,
    charges,
    pts,
    moments,
    feats,
    padded,
    kernels,
    basis,
    transfer,
    coupling,
    branch_t,
    branch_c,
    ladder,
    level,
    core_out,
    core_in,
    line_out,
    line_in,
    column_own,
    column_out,
    column_in,
    arrived,
    far,
    spread,
    norms,
    leaf_local,
    out_buf,
    load_sem,
    store_sem,
    send_sem,
    recv_sem,
):
    me = lax.axis_index("box")

    def other(distance):
        return lax.rem(me + distance + devices, devices)

    def flipped(pattern):
        return lax.bitwise_xor(me, pattern)

    odd_core = lax.rem(me, 2)
    sibling = me + 1 - 2 * odd_core

    def third(height):
        odd = lax.rem(lax.div(me, 1 << height), 2)
        return other((3 - 6 * odd) * (1 << height))

    def remote(index, src, dst, device):
        return pltpu.make_async_remote_copy(
            src_ref=src,
            dst_ref=dst,
            send_sem=send_sem.at[index],
            recv_sem=recv_sem.at[index],
            device_id=(device,),
            device_id_type=MESH,
        )

    barrier = pltpu.get_barrier_semaphore()
    partners = [other(s * (1 << k)) for k in range(LEVELS) for s in (1, -1)]
    partners += [other(devices // 2)] + [third(h) for h in range(LEVELS)]
    partners += [flipped(pattern) for pattern in PAIR]
    for partner in partners:
        pl.semaphore_signal(barrier, inc=1, device_id=(partner,), device_id_type=MESH)

    loads = []

    def load(src, dst):
        copy = pltpu.make_async_copy(src, dst, load_sem.at[len(loads)])
        copy.start()
        loads.append(copy)
        return copy

    load_points = [load(points.at[:, pl.ds(i * PTS, PTS)], pts.at[OWN + i]) for i in range(LEAF)]
    load_charges = [
        load(sources.at[:, pl.ds(i * PTS, PTS)], charges.at[OWN + i]) for i in range(LEAF)
    ]
    load_basis = load(basis_in, basis)
    load_transfer = load(leaf_transfer_in.at[0], transfer)
    load_branch_t = load(branch_transfer_in.at[0], branch_t)
    load_branch_c = load(branch_coupling_in.at[0], branch_c)
    load_coupling = load(coupling_in, coupling)

    def edge(base, buf, which):
        distance, first, count = EDGES[which]
        return remote(
            base + which,
            buf.at[pl.ds(OWN + first, count)],
            buf.at[pl.ds(OWN + first - LEAF * distance, count)],
            other(distance),
        )

    def window(which):
        if which == 0:
            return remote(
                I_WIN,
                charges.at[pl.ds(OWN, LEAF)],
                charges.at[pl.ds(4 + 16 * odd_core, LEAF)],
                sibling,
            )
        first, there = 8 + 12 * odd_core, 28 * odd_core
        return remote(
            I_WIN + 1, charges.at[pl.ds(first, 4)], charges.at[pl.ds(there, 4)], sibling
        )

    def ahead(k):
        leaf = lax.rem(k + 4 * odd_core, LEAF)
        return remote(
            I_WIN + 2 + k,
            charges.at[pl.ds(OWN + leaf, 1)],
            charges.at[pl.ds(leaf + 20 - 16 * odd_core, 1)],
            other(2 * odd_core - 1),
        )

    def behind(k):
        return remote(
            I_WIN + 10 + k,
            charges.at[pl.ds(OWN + 4 - 4 * odd_core + k, 1)],
            charges.at[pl.ds(28 * odd_core + k, 1)],
            other(2 - 4 * odd_core),
        )

    def core_copy():
        return remote(I_CORE, core_out, core_in, sibling)

    def line_copies():
        return [
            remote(I_LINE, line_out, line_in.at[pl.ds(0, 2)], flipped(2)),
            remote(I_LINE + 1, line_out.at[1], line_in.at[2], flipped(4)),
            remote(I_LINE + 2, line_out.at[1], line_in.at[3], flipped(6)),
        ]

    def column_first(k):
        return 0 if k == 1 else 1 if k < 4 else 2

    def column_copies():
        copies = []
        for k in range(1, 8):
            part = pl.ds(column_first(k), NEST - column_first(k))
            copies.append(
                remote(
                    I_COLUMN + k - 1, column_out.at[part], column_in.at[k - 1, part], flipped(8 * k)
                )
            )
        return copies

    def far_copies(height):
        step = 1 << height
        copies = []
        for slot, device in ((0, other(2 * step)), (1, other(-2 * step)), (2, third(height))):
            if height == LEVELS - 1 and slot == 1:
                continue
            copies.append(
                remote(I_FAR + 3 * height + slot, level.at[height], arrived.at[height, slot], device)
            )
        return copies

    def half(height):
        bit = lax.rem(lax.div(me, 1 << height), 2)
        joined = branch_t[height].astype(F32)
        return jnp.where(bit == 1, joined[:, RANK:], joined[:, :RANK]).astype(BF16)

    for copy in load_points:
        copy.wait()
    pl.semaphore_wait(barrier, len(partners))
    for which in range(N_EDGE):
        edge(I_PTS, pts, which).start()
    for copy in load_charges:
        copy.wait()
    ahead(0).start()
    ahead(1).start()
    window(0).start()

    load_basis.wait()
    load_transfer.wait()
    load_branch_t.wait()
    for i in range(LEAF):
        moments[OWN + i] = lax.dot_general(
            basis[i], charges[OWN + i], (((1,), (1,)), ((), ())), preferred_element_type=F32
        ).astype(BF16)
    base = jnp.dot(
        transfer[...],
        moments[pl.ds(OWN, LEAF)].reshape(LEAF * RANK, RHS),
        preferred_element_type=F32,
    )
    for nest in range(2):
        first, second, last = (half(NEST * nest + i) for i in range(NEST))
        two = jnp.dot(second, first, preferred_element_type=F32)
        three = exact_dot(last, two)
        high, low = halves(rows([first.astype(F32), two, three]))
        ladder[nest] = jnp.concatenate([high, low], axis=1)

    def climb(nest, x):
        high, low = halves(x)
        pair = ladder[nest]
        wide = jnp.concatenate([high, low], axis=1)
        r = jnp.dot(pair[:, :RANK], wide, preferred_element_type=F32)
        fine = jnp.dot(pair[:, RANK:], high, preferred_element_type=F32)
        return (r[:, :RHS] + r[:, RHS:] + fine).reshape(NEST, RANK, RHS)

    def descend(nest, x):
        wide = jnp.concatenate(halves(x), axis=1)
        r = lax.dot_general(
            ladder[nest], wide, (((0,), (0,)), ((), ())), preferred_element_type=F32
        )
        return r[:RANK, :RHS] + r[:RANK, RHS:] + r[RANK:, :RHS]

    core_out[...] = climb(0, base)
    level[0] = base.astype(BF16)
    core_copy().start()
    ahead(2).start()
    ahead(3).start()

    def core_step():
        core_copy().wait_recv()
        level[1] = (core_out[0] + core_in[0]).astype(BF16)
        line_out[...] = core_out[pl.ds(1, 2)] + core_in[pl.ds(1, 2)]
        for copy in line_copies():
            copy.start()

    def prepare(slot):
        x = rows([pts[slot], jnp.zeros((5, PTS), F32)])
        padded[slot] = x
        packed, own_norm = features((x - x[:, 0:1]) * SCALE, True)
        feats[slot] = packed.T.astype(BF16)
        apart = (x[0:3] - pts[OWN][:, 0:1]) * SCALE
        apart_norm = jnp.sum(apart * apart, axis=0, keepdims=True) * FAR_SCALE
        norms[pl.ds(slot, 1)] = jnp.maximum(own_norm, apart_norm)

    def prepare_pair(i, carry):
        prepare(2 * i)
        prepare(2 * i + 1)
        return carry

    lax.fori_loop(OWN // 2, (OWN + LEAF) // 2, prepare_pair, 0)
    core_step()
    for which in range(N_EDGE):
        edge(I_PTS, pts, which).wait_recv()
    lax.fori_loop(0, OWN // 2, prepare_pair, 0)
    lax.fori_loop((OWN + LEAF) // 2, SLOTS // 2, prepare_pair, 0)

    def slot_of(entry):
        return jnp.clip(entry - me * LEAF + OWN, 0, SLOTS - 1)

    def build(leaf, column):
        slot = slot_of(near_list[leaf, column])
        target = (padded[OWN + leaf] - padded[slot][:, 0:1]) * SCALE
        packed, _ = features(target, False)
        squared = jnp.dot(feats[slot], packed.astype(BF16), preferred_element_type=F32)
        kernels[leaf * NEAR + column] = lax.rsqrt(
            jnp.maximum(squared, SOFT * SCALE * SCALE)
        ).astype(BF16)

    def line_step():
        for copy in line_copies():
            copy.wait_recv()
        level[2] = (line_out[0] + line_in[0]).astype(BF16)
        third_level = (line_out[1] + line_in[1]) + (line_in[2] + line_in[3])
        level[3] = third_level.astype(BF16)
        column_own[...] = climb(1, third_level)
        column_out[...] = column_own[...].astype(BF16)
        for copy in column_copies():
            copy.start()
        for height in (3, 2, 1, 0):
            for copy in far_copies(height):
                copy.start()

    def column_step():
        for copy in column_copies():
            copy.wait_recv()
        for i in range(NEST):
            total = column_own[i]
            for k in range(1, 8):
                if column_first(k) <= i:
                    total += column_in[k - 1, i].astype(F32)
            level[NEST + 1 + i] = total.astype(BF16)
        for height in (6, 5, 4):
            for copy in far_copies(height):
                copy.start()

    def pass_step():
        for k in range(4):
            ahead(k).wait_recv()
        window(1).start()

    def moments_step():
        for which in range(N_EDGE):
            edge(I_MOM, moments, which).start()

    def far_step(height):
        for copy in far_copies(height):
            copy.wait_recv()
        index = lax.div(me, 1 << height)
        total = devices >> height
        odd = lax.rem(index, 2)

        def kept(slot, usable):
            block = arrived[height, slot]
            return jnp.where(usable, block, jnp.zeros_like(block))

        last = 0 if height == LEVELS - 1 else 1
        stack = rows(
            [
                kept(2, (odd == 1) & (index >= 3)),
                kept(0, index >= 2),
                kept(last, index + 2 < total),
                kept(2, (odd == 0) & (index + 3 < total)),
            ]
        )
        far[pl.ds(height * RANK, RANK)] = jnp.dot(
            branch_c[height], stack, preferred_element_type=F32
        )

    def down_step():
        upper = descend(1, far[pl.ds((NEST + 1) * RANK, NEST * RANK)])
        far[pl.ds(NEST * RANK, RANK)] += upper
        local = far[pl.ds(0, RANK)] + descend(0, far[pl.ds(RANK, NEST * RANK)])
        wide = jnp.concatenate(halves(local), axis=1)
        spread_both = lax.dot_general(
            transfer[...], wide, (((0,), (0,)), ((), ())), preferred_element_type=F32
        )
        spread[...] = (spread_both[:, :RHS] + spread_both[:, RHS:]).reshape(LEAF, RANK, RHS)

    def near_group(group, carry):
        leaf = lax.div(group, NEAR // GROUP)
        first = lax.rem(group, NEAR // GROUP) * GROUP
        for u in range(GROUP):
            build(leaf, first + u)
        @pl.when(group < 2)
        def _():
            ahead(4 + group).start()

        @pl.when(group == 2)
        def _():
            ahead(6).start()
            ahead(7).start()

        @pl.when((group >= 3) & (group < 5))
        def _():
            behind(2 * group - 6).start()
            behind(2 * group - 5).start()

        for step, at in (
            (line_step, LINE_AT),
            (pass_step, PASS_AT),
            (column_step, COLUMN_AT),
            (moments_step, MOMENTS_AT),
            (down_step, DOWN_AT),
        ):

            @pl.when(group == at)
            def _():
                step()

        for height, at in enumerate(FAR_AT):

            @pl.when(group == at)
            def _():
                if height == 0:
                    load_branch_c.wait()
                far_step(height)

        return carry

    lax.fori_loop(0, LEAF * NEAR // GROUP, near_group, 0)

    load_coupling.wait()
    for which in range(N_EDGE):
        edge(I_MOM, moments, which).wait_recv()
    window(0).wait_recv()
    window(1).wait_recv()
    for k in range(4):
        ahead(4 + k).wait_recv()
        behind(k).wait_recv()
    keep = [
        pltpu.make_async_copy(charges, charges_out, store_sem.at[2]),
        pltpu.make_async_copy(pts, points_out, store_sem.at[3]),
        pltpu.make_async_copy(norms, norms_out, store_sem.at[4]),
    ]
    for copy in keep:
        copy.start()

    def out_copy(leaf, buf):
        return pltpu.make_async_copy(
            out_buf.at[buf], field.at[:, pl.ds(pl.multiple_of(leaf * PTS, PTS), PTS)], store_sem.at[buf]
        )

    def finish(leaf, buf):
        blocks = []
        for j in range(FAR):
            block = moments[slot_of(far_list[j, leaf])]
            blocks.append(jnp.where(j < far_count[leaf], block.astype(F32), 0.0).astype(BF16))
        here = jnp.dot(coupling[leaf], rows(blocks), preferred_element_type=F32) + spread[leaf]
        here = here.astype(BF16)
        leaf_local[leaf] = here
        total = jnp.zeros((RHS, PTS), F32)
        for j in range(NEAR):
            block = charges[slot_of(near_list[leaf, j])]
            block = jnp.where(j < near_count[leaf], block, jnp.zeros_like(block))
            total += jnp.dot(block, kernels[leaf * NEAR + j], preferred_element_type=F32)
        out_buf[buf] = total + lax.dot_general(
            here, basis[leaf], (((0,), (0,)), ((), ())), preferred_element_type=F32
        )
        out_copy(leaf, buf).start()

    def finish_pair(i, carry):
        for buf in range(2):

            @pl.when(i > 0)
            def _():
                out_copy(2 * i - 2 + buf, buf).wait()

            finish(2 * i + buf, buf)
        return carry

    lax.fori_loop(0, LEAF // 2, finish_pair, 0)
    out_copy(LEAF - 2, 0).wait()
    out_copy(LEAF - 1, 1).wait()
    keep.append(pltpu.make_async_copy(leaf_local, leaf_local_out, store_sem.at[5]))
    keep[-1].start()
    for copy in keep:
        copy.wait()
    for which in range(N_EDGE):
        edge(I_PTS, pts, which).wait_send()
        edge(I_MOM, moments, which).wait_send()
    window(0).wait_send()
    window(1).wait_send()
    for k in range(8):
        ahead(k).wait_send()
    for k in range(4):
        behind(k).wait_send()
    for copy in [core_copy()] + line_copies() + column_copies():
        copy.wait_send()
    for height in range(LEVELS):
        for copy in far_copies(height):
            copy.wait_send()


N_LOAD = 2 * LEAF + 5


def tree(devices, *operands):
    any_spec = pl.BlockSpec(memory_space=pl.ANY)
    smem_spec = pl.BlockSpec(memory_space=pltpu.SMEM)
    return pl.pallas_call(
        functools.partial(tree_kernel, devices),
        out_shape=(
            jax.ShapeDtypeStruct((RHS, LEAF * PTS), F32),
            jax.ShapeDtypeStruct((LEAF, RANK, RHS), BF16),
            jax.ShapeDtypeStruct((SLOTS, PTS), F32),
            jax.ShapeDtypeStruct((SLOTS, RHS, PTS), BF16),
            jax.ShapeDtypeStruct((SLOTS, 3, PTS), F32),
        ),
        in_specs=[smem_spec] * 4 + [any_spec] * 7,
        out_specs=(any_spec,) * 5,
        scratch_shapes=[
            pltpu.VMEM((SLOTS, RHS, PTS), BF16),
            pltpu.VMEM((SLOTS, 3, PTS), F32),
            pltpu.VMEM((SLOTS, RANK, RHS), BF16),
            pltpu.VMEM((SLOTS, PTS, FEAT), BF16),
            pltpu.VMEM((SLOTS, 8, PTS), F32),
            pltpu.VMEM((LEAF * NEAR, PTS, PTS), BF16),
            pltpu.VMEM((LEAF, RANK, PTS), BF16),
            pltpu.VMEM((RANK, LEAF * RANK), BF16),
            pltpu.VMEM((LEAF, RANK, FAR * RANK), BF16),
            pltpu.VMEM((UP, RANK, 2 * RANK), BF16),
            pltpu.VMEM((LEVELS, RANK, 4 * RANK), BF16),
            pltpu.VMEM((2, NEST * RANK, 2 * RANK), BF16),
            pltpu.VMEM((LEVELS, RANK, RHS), BF16),
            pltpu.VMEM((NEST, RANK, RHS), F32),
            pltpu.VMEM((NEST, RANK, RHS), F32),
            pltpu.VMEM((2, RANK, RHS), F32),
            pltpu.VMEM((4, RANK, RHS), F32),
            pltpu.VMEM((NEST, RANK, RHS), F32),
            pltpu.VMEM((NEST, RANK, RHS), BF16),
            pltpu.VMEM((7, NEST, RANK, RHS), BF16),
            pltpu.VMEM((LEVELS, 3, RANK, RHS), BF16),
            pltpu.VMEM((LEVELS * RANK, RHS), F32),
            pltpu.VMEM((LEAF, RANK, RHS), F32),
            pltpu.VMEM((SLOTS, PTS), F32),
            pltpu.VMEM((LEAF, RANK, RHS), BF16),
            pltpu.VMEM((2, RHS, PTS), F32),
            pltpu.SemaphoreType.DMA((N_LOAD,)),
            pltpu.SemaphoreType.DMA((6,)),
            pltpu.SemaphoreType.DMA((N_MSG,)),
            pltpu.SemaphoreType.DMA((N_MSG,)),
        ],
        compiler_params=pltpu.CompilerParams(
            collective_id=0, has_side_effects=True, vmem_limit_bytes=66_000_000
        ),
        name="tree",
    )(*operands)


def result_kernel(
    near_list, near_count, norms, fast, leaf_local, charges, points, basis, field,
    buf, charge_buf, point_buf, local_buf, basis_buf, norm_buf, in_sem, out_sem, sem,
):
    def cols(leaf):
        return pl.ds(leaf * PTS, PTS)

    reads = [
        pltpu.make_async_copy(fast.at[:, cols(i)], buf.at[i], in_sem.at[i]) for i in range(LEAF)
    ]
    writes = [
        pltpu.make_async_copy(buf.at[i], field.at[:, cols(i)], out_sem.at[i]) for i in range(LEAF)
    ]
    get_norms = pltpu.make_async_copy(norms, norm_buf, sem)
    get_norms.start()
    for copy in reads:
        copy.start()
    get_norms.wait()
    direct = jnp.max(jnp.where(norm_buf[...] <= EXTENT, 0.0, 1.0)) > 0.0

    @pl.when(jnp.logical_not(direct))
    def _():
        for read, write in zip(reads, writes):
            read.wait()
            write.start()
        for write in writes:
            write.wait()

    @pl.when(direct)
    def _():
        me = lax.axis_index("box")
        for read in reads:
            read.wait()

        def fetch(src, dst):
            copy = pltpu.make_async_copy(src, dst, sem)
            copy.start()
            copy.wait()

        fetch(points, point_buf)
        fetch(leaf_local, local_buf)
        fetch(basis, basis_buf)

        def one(leaf, carry):
            buf[0] = lax.dot_general(
                local_buf[leaf], basis_buf[leaf], (((0,), (0,)), ((), ())), preferred_element_type=F32
            )
            target = point_buf[OWN + leaf]

            def pair(j, inner):
                slot = jnp.clip(near_list[leaf, j] - me * LEAF + OWN, 0, SLOTS - 1)
                fetch(charges.at[slot], charge_buf)
                column = point_buf[slot].T
                squared = SOFT
                for axis in range(3):
                    gap = column[:, axis : axis + 1] - target[axis : axis + 1]
                    squared = squared + gap * gap
                block = (INV * lax.rsqrt(squared)).astype(BF16)
                buf[0] += jnp.dot(charge_buf[...], block, preferred_element_type=F32)
                return inner

            lax.fori_loop(0, near_count[leaf], pair, 0)
            fetch(buf.at[0], field.at[:, pl.ds(pl.multiple_of(leaf * PTS, PTS), PTS)])
            return carry

        lax.fori_loop(0, LEAF, one, 0)


def result(*operands):
    any_spec = pl.BlockSpec(memory_space=pl.ANY)
    smem_spec = pl.BlockSpec(memory_space=pltpu.SMEM)
    return pl.pallas_call(
        result_kernel,
        out_shape=jax.ShapeDtypeStruct((RHS, LEAF * PTS), F32),
        in_specs=[smem_spec] * 2 + [any_spec] * 6,
        out_specs=any_spec,
        scratch_shapes=[
            pltpu.VMEM((LEAF, RHS, PTS), F32),
            pltpu.VMEM((RHS, PTS), BF16),
            pltpu.VMEM((SLOTS, 3, PTS), F32),
            pltpu.VMEM((LEAF, RANK, RHS), BF16),
            pltpu.VMEM((LEAF, RANK, PTS), BF16),
            pltpu.VMEM((SLOTS, PTS), F32),
            pltpu.SemaphoreType.DMA((LEAF,)),
            pltpu.SemaphoreType.DMA((LEAF,)),
            pltpu.SemaphoreType.DMA,
        ],
        name="result",
    )(*operands)


def on_device(
    sources, points, near_list, near_count, far_list, far_count,
    leaf_basis, leaf_transfer, leaf_coupling, branch_transfer, branch_coupling,
):
    devices = lax.axis_size("box")
    fast, leaf_local, norms, charges, window_points = tree(
        devices, near_list, near_count, far_list.T, far_count, sources, points,
        leaf_basis, leaf_transfer, leaf_coupling, branch_transfer, branch_coupling,
    )
    return result(
        near_list, near_count, norms, fast, leaf_local, charges, window_points, leaf_basis
    )


def solution(mesh):
    placed = (
        P(None, "box"),
        P(None, "box"),
        P("box", None),
        P("box"),
        P("box", None),
        P("box"),
        P("box", None, None),
        P("box", None, None),
        P("box", None, None),
        P("box", None, None, None),
        P("box", None, None, None),
    )
    return jax.shard_map(
        on_device, mesh=mesh, in_specs=placed, out_specs=P(None, "box"), check_vma=False
    )
```

```python
import functools

import jax
import jax.numpy as jnp
from jax import lax
from jax.experimental import pallas as pl
from jax.experimental.pallas import tpu as pltpu
from jax.sharding import PartitionSpec as P

F32 = jnp.float32
BF16 = jnp.bfloat16
SOFT = 0.25
INV = 0.07957747154594767
SCALE = 1.0 / INV
EXTENT = 1024.0 * SCALE * SCALE
FAR_SCALE = 1e-27
LEAF = 8
PTS = 512
RANK = 64
RHS = 128
NEAR = 12
FAR = 4
REACH = 12
SLOTS = LEAF + 2 * REACH
OWN = REACH
UP = 6
LEVELS = 7
FEAT = 48
GROUP = 12
MESH = pl.DeviceIdType.MESH

EDGES = ((1, 0, 8), (-1, 0, 8), (2, 4, 4), (-2, 0, 4))
N_EDGE = len(EDGES)
NEST = 3
PAIR = (6, 24, 40, 48, 56)
I_PTS = 0
I_MOM = I_PTS + N_EDGE
I_WIN = I_MOM + N_EDGE
N_WIN = 14
I_CORE = I_WIN + N_WIN
I_LINE = I_CORE + 1
I_COLUMN = I_LINE + 3
I_FAR = I_COLUMN + 7
N_MSG = I_FAR + 3 * LEVELS

LINE_AT, PASS_AT, COLUMN_AT, MOMENTS_AT, DOWN_AT = 0, 2, 2, 5, 7
FAR_AT = (3, 3, 5, 4, 5, 6, 6)


def split3(x):
    a = x.astype(BF16)
    r = x - a.astype(F32)
    b = r.astype(BF16)
    return a, b, (r - b.astype(F32)).astype(BF16)


def rows(parts):
    return jnp.concatenate(parts, axis=0)


def halves(x):
    high = x.astype(BF16)
    return high, (x - high.astype(F32)).astype(BF16)


def features(x, of_source):
    row = lax.broadcasted_iota(jnp.int32, x.shape, 0)
    n = jnp.sum(x * x, axis=0, keepdims=True)
    a, b, c = (v.astype(F32) for v in split3(x if of_source else -2.0 * x))
    n0, n1, n2 = (v.astype(F32) for v in split3(n + SOFT * SCALE * SCALE if of_source else n))
    norm = jnp.where(row == 3, n0, jnp.where(row == 4, n1, jnp.where(row == 5, n2, 0.0)))
    ones = jnp.where((row >= 3) & (row < 6), 1.0, 0.0)
    if of_source:
        parts = [a + norm, b + ones, a, b, c, a]
    else:
        parts = [a + ones, a + norm, b, b, a, c]
    return rows(parts), n


def exact_dot(left, right):
    width = right.shape[1]
    both = jnp.dot(left, jnp.concatenate(halves(right), axis=1), preferred_element_type=F32)
    return both[:, :width] + both[:, width:]


def tree_kernel(
    devices,
    near_list,
    near_count,
    far_list,
    far_count,
    sources,
    points,
    basis_in,
    leaf_transfer_in,
    coupling_in,
    branch_transfer_in,
    branch_coupling_in,
    field,
    leaf_local_out,
    norms_out,
    charges_out,
    points_out,
    charges,
    pts,
    moments,
    feats,
    padded,
    kernels,
    basis,
    transfer,
    coupling,
    branch_t,
    branch_c,
    ladder,
    level,
    core_out,
    core_in,
    line_out,
    line_in,
    column_own,
    column_out,
    column_in,
    arrived,
    far,
    spread,
    norms,
    leaf_local,
    out_buf,
    load_sem,
    store_sem,
    send_sem,
    recv_sem,
):
    me = lax.axis_index("box")

    def other(distance):
        return lax.rem(me + distance + devices, devices)

    def flipped(pattern):
        return lax.bitwise_xor(me, pattern)

    odd_core = lax.rem(me, 2)
    sibling = me + 1 - 2 * odd_core

    def third(height):
        odd = lax.rem(lax.div(me, 1 << height), 2)
        return other((3 - 6 * odd) * (1 << height))

    def remote(index, src, dst, device):
        return pltpu.make_async_remote_copy(
            src_ref=src,
            dst_ref=dst,
            send_sem=send_sem.at[index],
            recv_sem=recv_sem.at[index],
            device_id=(device,),
            device_id_type=MESH,
        )

    barrier = pltpu.get_barrier_semaphore()
    partners = [other(s * (1 << k)) for k in range(LEVELS) for s in (1, -1)]
    partners += [other(devices // 2)] + [third(h) for h in range(LEVELS)]
    partners += [flipped(pattern) for pattern in PAIR]
    for partner in partners:
        pl.semaphore_signal(barrier, inc=1, device_id=(partner,), device_id_type=MESH)

    loads = []

    def load(src, dst):
        copy = pltpu.make_async_copy(src, dst, load_sem.at[len(loads)])
        copy.start()
        loads.append(copy)
        return copy

    load_points = [load(points.at[:, pl.ds(i * PTS, PTS)], pts.at[OWN + i]) for i in range(LEAF)]
    load_charges = [
        load(sources.at[:, pl.ds(i * PTS, PTS)], charges.at[OWN + i]) for i in range(LEAF)
    ]
    load_basis = load(basis_in, basis)
    load_transfer = load(leaf_transfer_in.at[0], transfer)
    load_branch_t = load(branch_transfer_in.at[0], branch_t)
    load_branch_c = load(branch_coupling_in.at[0], branch_c)
    load_coupling = load(coupling_in, coupling)

    def edge(base, buf, which):
        distance, first, count = EDGES[which]
        return remote(
            base + which,
            buf.at[pl.ds(OWN + first, count)],
            buf.at[pl.ds(OWN + first - LEAF * distance, count)],
            other(distance),
        )

    def window(which):
        if which == 0:
            return remote(
                I_WIN,
                charges.at[pl.ds(OWN, LEAF)],
                charges.at[pl.ds(4 + 16 * odd_core, LEAF)],
                sibling,
            )
        first, there = 8 + 12 * odd_core, 28 * odd_core
        return remote(
            I_WIN + 1, charges.at[pl.ds(first, 4)], charges.at[pl.ds(there, 4)], sibling
        )

    def ahead(k):
        leaf = lax.rem(k + 4 * odd_core, LEAF)
        return remote(
            I_WIN + 2 + k,
            charges.at[pl.ds(OWN + leaf, 1)],
            charges.at[pl.ds(leaf + 20 - 16 * odd_core, 1)],
            other(2 * odd_core - 1),
        )

    def behind(k):
        return remote(
            I_WIN + 10 + k,
            charges.at[pl.ds(OWN + 4 - 4 * odd_core + k, 1)],
            charges.at[pl.ds(28 * odd_core + k, 1)],
            other(2 - 4 * odd_core),
        )

    def core_copy():
        return remote(I_CORE, core_out, core_in, sibling)

    def line_copies():
        return [
            remote(I_LINE, line_out, line_in.at[pl.ds(0, 2)], flipped(2)),
            remote(I_LINE + 1, line_out.at[1], line_in.at[2], flipped(4)),
            remote(I_LINE + 2, line_out.at[1], line_in.at[3], flipped(6)),
        ]

    def column_first(k):
        return 0 if k == 1 else 1 if k < 4 else 2

    def column_copies():
        copies = []
        for k in range(1, 8):
            part = pl.ds(column_first(k), NEST - column_first(k))
            copies.append(
                remote(
                    I_COLUMN + k - 1, column_out.at[part], column_in.at[k - 1, part], flipped(8 * k)
                )
            )
        return copies

    def far_copies(height):
        step = 1 << height
        copies = []
        for slot, device in ((0, other(2 * step)), (1, other(-2 * step)), (2, third(height))):
            if height == LEVELS - 1 and slot == 1:
                continue
            copies.append(
                remote(I_FAR + 3 * height + slot, level.at[height], arrived.at[height, slot], device)
            )
        return copies

    def half(height):
        bit = lax.rem(lax.div(me, 1 << height), 2)
        joined = branch_t[height].astype(F32)
        return jnp.where(bit == 1, joined[:, RANK:], joined[:, :RANK]).astype(BF16)

    for copy in load_points:
        copy.wait()
    def prepare(slot):
        x = rows([pts[slot], jnp.zeros((5, PTS), F32)])
        padded[slot] = x
        packed, own_norm = features((x - x[:, 0:1]) * SCALE, True)
        feats[slot] = packed.T.astype(BF16)
        apart = (x[0:3] - pts[OWN][:, 0:1]) * SCALE
        apart_norm = jnp.sum(apart * apart, axis=0, keepdims=True) * FAR_SCALE
        norms[pl.ds(slot, 1)] = jnp.maximum(own_norm, apart_norm)

    def prepare_pair(i, carry):
        prepare(2 * i)
        prepare(2 * i + 1)
        return carry

    lax.fori_loop(OWN // 2, (OWN + LEAF) // 2, prepare_pair, 0)
    pl.semaphore_wait(barrier, len(partners))
    for which in range(N_EDGE):
        edge(I_PTS, pts, which).start()
    for copy in load_charges:
        copy.wait()
    ahead(0).start()
    ahead(1).start()
    window(0).start()

    load_basis.wait()
    load_transfer.wait()
    load_branch_t.wait()
    for i in range(LEAF):
        moments[OWN + i] = lax.dot_general(
            basis[i], charges[OWN + i], (((1,), (1,)), ((), ())), preferred_element_type=F32
        ).astype(BF16)
    base = jnp.dot(
        transfer[...],
        moments[pl.ds(OWN, LEAF)].reshape(LEAF * RANK, RHS),
        preferred_element_type=F32,
    )
    for nest in range(2):
        first, second, last = (half(NEST * nest + i) for i in range(NEST))
        two = jnp.dot(second, first, preferred_element_type=F32)
        three = exact_dot(last, two)
        high, low = halves(rows([first.astype(F32), two, three]))
        ladder[nest] = jnp.concatenate([high, low], axis=1)

    def climb(nest, x):
        high, low = halves(x)
        pair = ladder[nest]
        wide = jnp.concatenate([high, low], axis=1)
        r = jnp.dot(pair[:, :RANK], wide, preferred_element_type=F32)
        fine = jnp.dot(pair[:, RANK:], high, preferred_element_type=F32)
        return (r[:, :RHS] + r[:, RHS:] + fine).reshape(NEST, RANK, RHS)

    def descend(nest, x):
        wide = jnp.concatenate(halves(x), axis=1)
        r = lax.dot_general(
            ladder[nest], wide, (((0,), (0,)), ((), ())), preferred_element_type=F32
        )
        return r[:RANK, :RHS] + r[:RANK, RHS:] + r[RANK:, :RHS]

    core_out[...] = climb(0, base)
    level[0] = base.astype(BF16)
    core_copy().start()
    ahead(2).start()
    ahead(3).start()

    def core_step():
        core_copy().wait_recv()
        level[1] = (core_out[0] + core_in[0]).astype(BF16)
        line_out[...] = core_out[pl.ds(1, 2)] + core_in[pl.ds(1, 2)]
        for copy in line_copies():
            copy.start()

    core_step()
    for which in range(N_EDGE):
        edge(I_PTS, pts, which).wait_recv()
    lax.fori_loop(0, OWN // 2, prepare_pair, 0)
    lax.fori_loop((OWN + LEAF) // 2, SLOTS // 2, prepare_pair, 0)

    def slot_of(entry):
        return jnp.clip(entry - me * LEAF + OWN, 0, SLOTS - 1)

    def build(leaf, column):
        slot = slot_of(near_list[leaf, column])
        target = (padded[OWN + leaf] - padded[slot][:, 0:1]) * SCALE
        packed, _ = features(target, False)
        squared = jnp.dot(feats[slot], packed.astype(BF16), preferred_element_type=F32)
        kernels[leaf * NEAR + column] = lax.rsqrt(
            jnp.maximum(squared, SOFT * SCALE * SCALE)
        ).astype(BF16)

    def line_step():
        for copy in line_copies():
            copy.wait_recv()
        level[2] = (line_out[0] + line_in[0]).astype(BF16)
        third_level = (line_out[1] + line_in[1]) + (line_in[2] + line_in[3])
        level[3] = third_level.astype(BF16)
        column_own[...] = climb(1, third_level)
        column_out[...] = column_own[...].astype(BF16)
        for copy in column_copies():
            copy.start()
        for height in (3, 2, 1, 0):
            for copy in far_copies(height):
                copy.start()

    def column_step():
        for copy in column_copies():
            copy.wait_recv()
        for i in range(NEST):
            total = column_own[i]
            for k in range(1, 8):
                if column_first(k) <= i:
                    total += column_in[k - 1, i].astype(F32)
            level[NEST + 1 + i] = total.astype(BF16)
        for height in (6, 5, 4):
            for copy in far_copies(height):
                copy.start()

    def pass_step():
        for k in range(4):
            ahead(k).wait_recv()
        window(1).start()

    def moments_step():
        for which in range(N_EDGE):
            edge(I_MOM, moments, which).start()

    def far_step(height):
        for copy in far_copies(height):
            copy.wait_recv()
        index = lax.div(me, 1 << height)
        total = devices >> height
        odd = lax.rem(index, 2)

        def kept(slot, usable):
            block = arrived[height, slot]
            return jnp.where(usable, block, jnp.zeros_like(block))

        last = 0 if height == LEVELS - 1 else 1
        stack = rows(
            [
                kept(2, (odd == 1) & (index >= 3)),
                kept(0, index >= 2),
                kept(last, index + 2 < total),
                kept(2, (odd == 0) & (index + 3 < total)),
            ]
        )
        far[pl.ds(height * RANK, RANK)] = jnp.dot(
            branch_c[height], stack, preferred_element_type=F32
        )

    def down_step():
        upper = descend(1, far[pl.ds((NEST + 1) * RANK, NEST * RANK)])
        far[pl.ds(NEST * RANK, RANK)] += upper
        local = far[pl.ds(0, RANK)] + descend(0, far[pl.ds(RANK, NEST * RANK)])
        wide = jnp.concatenate(halves(local), axis=1)
        spread_both = lax.dot_general(
            transfer[...], wide, (((0,), (0,)), ((), ())), preferred_element_type=F32
        )
        spread[...] = (spread_both[:, :RHS] + spread_both[:, RHS:]).reshape(LEAF, RANK, RHS)

    def near_group(group, carry):
        leaf = lax.div(group, NEAR // GROUP)
        first = lax.rem(group, NEAR // GROUP) * GROUP
        for u in range(GROUP):
            build(leaf, first + u)
        @pl.when(group < 2)
        def _():
            ahead(4 + group).start()

        @pl.when(group == 2)
        def _():
            ahead(6).start()
            ahead(7).start()

        @pl.when((group >= 3) & (group < 5))
        def _():
            behind(2 * group - 6).start()
            behind(2 * group - 5).start()

        for step, at in (
            (line_step, LINE_AT),
            (pass_step, PASS_AT),
            (column_step, COLUMN_AT),
            (moments_step, MOMENTS_AT),
            (down_step, DOWN_AT),
        ):

            @pl.when(group == at)
            def _():
                step()

        for height, at in enumerate(FAR_AT):

            @pl.when(group == at)
            def _():
                if height == 0:
                    load_branch_c.wait()
                far_step(height)

        return carry

    lax.fori_loop(0, LEAF * NEAR // GROUP, near_group, 0)

    load_coupling.wait()
    for which in range(N_EDGE):
        edge(I_MOM, moments, which).wait_recv()
    window(0).wait_recv()
    window(1).wait_recv()
    for k in range(4):
        ahead(4 + k).wait_recv()
        behind(k).wait_recv()
    keep = [
        pltpu.make_async_copy(charges, charges_out, store_sem.at[2]),
        pltpu.make_async_copy(pts, points_out, store_sem.at[3]),
        pltpu.make_async_copy(norms, norms_out, store_sem.at[4]),
    ]
    for copy in keep:
        copy.start()

    def out_copy(leaf, buf):
        return pltpu.make_async_copy(
            out_buf.at[buf], field.at[:, pl.ds(pl.multiple_of(leaf * PTS, PTS), PTS)], store_sem.at[buf]
        )

    def finish(leaf, buf):
        blocks = []
        for j in range(FAR):
            block = moments[slot_of(far_list[j, leaf])]
            blocks.append(jnp.where(j < far_count[leaf], block.astype(F32), 0.0).astype(BF16))
        here = jnp.dot(coupling[leaf], rows(blocks), preferred_element_type=F32) + spread[leaf]
        here = here.astype(BF16)
        leaf_local[leaf] = here
        total = jnp.zeros((RHS, PTS), F32)
        for j in range(NEAR):
            block = charges[slot_of(near_list[leaf, j])]
            block = jnp.where(j < near_count[leaf], block, jnp.zeros_like(block))
            total += jnp.dot(block, kernels[leaf * NEAR + j], preferred_element_type=F32)
        out_buf[buf] = total + lax.dot_general(
            here, basis[leaf], (((0,), (0,)), ((), ())), preferred_element_type=F32
        )
        out_copy(leaf, buf).start()

    def finish_pair(i, carry):
        for buf in range(2):

            @pl.when(i > 0)
            def _():
                out_copy(2 * i - 2 + buf, buf).wait()

            finish(2 * i + buf, buf)
        return carry

    lax.fori_loop(0, LEAF // 2, finish_pair, 0)
    out_copy(LEAF - 2, 0).wait()
    out_copy(LEAF - 1, 1).wait()
    keep.append(pltpu.make_async_copy(leaf_local, leaf_local_out, store_sem.at[5]))
    keep[-1].start()
    for copy in keep:
        copy.wait()
    for which in range(N_EDGE):
        edge(I_PTS, pts, which).wait_send()
        edge(I_MOM, moments, which).wait_send()
    window(0).wait_send()
    window(1).wait_send()
    for k in range(8):
        ahead(k).wait_send()
    for k in range(4):
        behind(k).wait_send()
    for copy in [core_copy()] + line_copies() + column_copies():
        copy.wait_send()
    for height in range(LEVELS):
        for copy in far_copies(height):
            copy.wait_send()


N_LOAD = 2 * LEAF + 5


def tree(devices, *operands):
    any_spec = pl.BlockSpec(memory_space=pl.ANY)
    smem_spec = pl.BlockSpec(memory_space=pltpu.SMEM)
    return pl.pallas_call(
        functools.partial(tree_kernel, devices),
        out_shape=(
            jax.ShapeDtypeStruct((RHS, LEAF * PTS), F32),
            jax.ShapeDtypeStruct((LEAF, RANK, RHS), BF16),
            jax.ShapeDtypeStruct((SLOTS, PTS), F32),
            jax.ShapeDtypeStruct((SLOTS, RHS, PTS), BF16),
            jax.ShapeDtypeStruct((SLOTS, 3, PTS), F32),
        ),
        in_specs=[smem_spec] * 4 + [any_spec] * 7,
        out_specs=(any_spec,) * 5,
        scratch_shapes=[
            pltpu.VMEM((SLOTS, RHS, PTS), BF16),
            pltpu.VMEM((SLOTS, 3, PTS), F32),
            pltpu.VMEM((SLOTS, RANK, RHS), BF16),
            pltpu.VMEM((SLOTS, PTS, FEAT), BF16),
            pltpu.VMEM((SLOTS, 8, PTS), F32),
            pltpu.VMEM((LEAF * NEAR, PTS, PTS), BF16),
            pltpu.VMEM((LEAF, RANK, PTS), BF16),
            pltpu.VMEM((RANK, LEAF * RANK), BF16),
            pltpu.VMEM((LEAF, RANK, FAR * RANK), BF16),
            pltpu.VMEM((UP, RANK, 2 * RANK), BF16),
            pltpu.VMEM((LEVELS, RANK, 4 * RANK), BF16),
            pltpu.VMEM((2, NEST * RANK, 2 * RANK), BF16),
            pltpu.VMEM((LEVELS, RANK, RHS), BF16),
            pltpu.VMEM((NEST, RANK, RHS), F32),
            pltpu.VMEM((NEST, RANK, RHS), F32),
            pltpu.VMEM((2, RANK, RHS), F32),
            pltpu.VMEM((4, RANK, RHS), F32),
            pltpu.VMEM((NEST, RANK, RHS), F32),
            pltpu.VMEM((NEST, RANK, RHS), BF16),
            pltpu.VMEM((7, NEST, RANK, RHS), BF16),
            pltpu.VMEM((LEVELS, 3, RANK, RHS), BF16),
            pltpu.VMEM((LEVELS * RANK, RHS), F32),
            pltpu.VMEM((LEAF, RANK, RHS), F32),
            pltpu.VMEM((SLOTS, PTS), F32),
            pltpu.VMEM((LEAF, RANK, RHS), BF16),
            pltpu.VMEM((2, RHS, PTS), F32),
            pltpu.SemaphoreType.DMA((N_LOAD,)),
            pltpu.SemaphoreType.DMA((6,)),
            pltpu.SemaphoreType.DMA((N_MSG,)),
            pltpu.SemaphoreType.DMA((N_MSG,)),
        ],
        compiler_params=pltpu.CompilerParams(
            collective_id=0, has_side_effects=True, vmem_limit_bytes=66_000_000
        ),
        name="tree",
    )(*operands)


def result_kernel(
    near_list, near_count, norms, fast, leaf_local, charges, points, basis, field,
    buf, charge_buf, point_buf, local_buf, basis_buf, norm_buf, in_sem, out_sem, sem,
):
    def cols(leaf):
        return pl.ds(leaf * PTS, PTS)

    reads = [
        pltpu.make_async_copy(fast.at[:, cols(i)], buf.at[i], in_sem.at[i]) for i in range(LEAF)
    ]
    writes = [
        pltpu.make_async_copy(buf.at[i], field.at[:, cols(i)], out_sem.at[i]) for i in range(LEAF)
    ]
    get_norms = pltpu.make_async_copy(norms, norm_buf, sem)
    get_norms.start()
    for copy in reads:
        copy.start()
    get_norms.wait()
    direct = jnp.max(jnp.where(norm_buf[...] <= EXTENT, 0.0, 1.0)) > 0.0

    @pl.when(jnp.logical_not(direct))
    def _():
        for read, write in zip(reads, writes):
            read.wait()
            write.start()
        for write in writes:
            write.wait()

    @pl.when(direct)
    def _():
        me = lax.axis_index("box")
        for read in reads:
            read.wait()

        def fetch(src, dst):
            copy = pltpu.make_async_copy(src, dst, sem)
            copy.start()
            copy.wait()

        fetch(points, point_buf)
        fetch(leaf_local, local_buf)
        fetch(basis, basis_buf)

        def one(leaf, carry):
            buf[0] = lax.dot_general(
                local_buf[leaf], basis_buf[leaf], (((0,), (0,)), ((), ())), preferred_element_type=F32
            )
            target = point_buf[OWN + leaf]

            def pair(j, inner):
                slot = jnp.clip(near_list[leaf, j] - me * LEAF + OWN, 0, SLOTS - 1)
                fetch(charges.at[slot], charge_buf)
                column = point_buf[slot].T
                squared = SOFT
                for axis in range(3):
                    gap = column[:, axis : axis + 1] - target[axis : axis + 1]
                    squared = squared + gap * gap
                block = (INV * lax.rsqrt(squared)).astype(BF16)
                buf[0] += jnp.dot(charge_buf[...], block, preferred_element_type=F32)
                return inner

            lax.fori_loop(0, near_count[leaf], pair, 0)
            fetch(buf.at[0], field.at[:, pl.ds(pl.multiple_of(leaf * PTS, PTS), PTS)])
            return carry

        lax.fori_loop(0, LEAF, one, 0)


def result(*operands):
    any_spec = pl.BlockSpec(memory_space=pl.ANY)
    smem_spec = pl.BlockSpec(memory_space=pltpu.SMEM)
    return pl.pallas_call(
        result_kernel,
        out_shape=jax.ShapeDtypeStruct((RHS, LEAF * PTS), F32),
        in_specs=[smem_spec] * 2 + [any_spec] * 6,
        out_specs=any_spec,
        scratch_shapes=[
            pltpu.VMEM((LEAF, RHS, PTS), F32),
            pltpu.VMEM((RHS, PTS), BF16),
            pltpu.VMEM((SLOTS, 3, PTS), F32),
            pltpu.VMEM((LEAF, RANK, RHS), BF16),
            pltpu.VMEM((LEAF, RANK, PTS), BF16),
            pltpu.VMEM((SLOTS, PTS), F32),
            pltpu.SemaphoreType.DMA((LEAF,)),
            pltpu.SemaphoreType.DMA((LEAF,)),
            pltpu.SemaphoreType.DMA,
        ],
        name="result",
    )(*operands)


def on_device(
    sources, points, near_list, near_count, far_list, far_count,
    leaf_basis, leaf_transfer, leaf_coupling, branch_transfer, branch_coupling,
):
    devices = lax.axis_size("box")
    fast, leaf_local, norms, charges, window_points = tree(
        devices, near_list, near_count, far_list.T, far_count, sources, points,
        leaf_basis, leaf_transfer, leaf_coupling, branch_transfer, branch_coupling,
    )
    return result(
        near_list, near_count, norms, fast, leaf_local, charges, window_points, leaf_basis
    )


def solution(mesh):
    placed = (
        P(None, "box"),
        P(None, "box"),
        P("box", None),
        P("box"),
        P("box", None),
        P("box"),
        P("box", None, None),
        P("box", None, None),
        P("box", None, None),
        P("box", None, None, None),
        P("box", None, None, None),
    )
    return jax.shard_map(
        on_device, mesh=mesh, in_specs=placed, out_specs=P(None, "box"), check_vma=False
    )
```
